256 devices in a mesh: ctx: 64 (over x, z, core), cache: 4 (over y).
Axes of the slice: x: 4, y: 4, z: 8, core: 2. Of those that a mesh axis runs over, the one named last changes fastest.
Arguments:
- queries: bfloat16 [8192, 8192], P('ctx'), may hold values from -6 to 6
- keys: bfloat16 [192, 64, 8192], P('cache', None, 'ctx'), may hold values from -6 to 6
- values: bfloat16 [192, 64, 8192], P('cache', None, 'ctx'), may hold values from -6 to 6
- block_imgs: int32 [32, 16], replicated, may hold values from 0 to 192, as said below
- img_req: int32 [192], replicated, may hold values from 0 to 31, as said below
- req_start: int32 [32], replicated, may hold values from 0 to 8064, as said below
Outputs:
- attended: bfloat16 [8192, 8192], P('ctx')
The draws below stay inside these ranges and needn't reach their ends.
Inputs may be any that keep to these rules, and one draw needn't show every extreme that they name: `block_imgs`: row b holds in slots 0 to 7 the images of request b - 1 (empty for b = 0) and in slots 8 to 15 those of request b; a request without images leaves its slots empty; the value 192 marks an empty slot; some rows are full. `img_req`: every request with images owns exactly 8 of them; 8 requests own none; the first and the last request own images. req_start[0] = 0, and request r begins inside text block r after the block's first token, at most 128 tokens in, so block b holds the tail of request b - 1 and the head of request b.
All inputs are finite; a program needn't handle non-finite values.
Results may differ from the reference program's by a relative error of at most 0.005.
Values may be sent and summed in bfloat16 or wider, within the bound.
A program may use at most 128 MiB of HBM per device.

```python
import math
import jax
import jax.numpy as jnp
from jax import lax

H = 64
HD = 128
LAT = 64
BLOCK = 256
IMG_REQ = 8
TOKENS = 8192
NBLK = 32
REQS = 32
IMGS = 192
MAXVIS = 16


def layout(key):
    base_key = jax.random.fold_in(key, 11)
    key_offsets, key_requests, key_images = jax.random.split(base_key, 3)
    request_ids = jnp.arange(REQS, dtype=jnp.int32)
    offsets = jax.random.randint(key_offsets, (REQS,), 1, BLOCK // 2 + 1)
    offsets = jnp.where(request_ids == REQS - 1, BLOCK // 2, offsets)
    offsets = jnp.where(request_ids == 0, 0, offsets)
    req_start = (request_ids * BLOCK + offsets).astype(jnp.int32)
    middle_perm = jax.random.permutation(key_requests, REQS - 2).astype(jnp.int32)
    middle_has = (middle_perm >= REQS // 4).astype(jnp.int32)
    has_images = jnp.concatenate([jnp.ones((1,), jnp.int32), middle_has, jnp.ones((1,), jnp.int32)])
    request_order = jnp.argsort((1 - has_images) * REQS + request_ids, stable=True).astype(jnp.int32)
    image_ids = jnp.arange(IMGS, dtype=jnp.int32)
    image_owner = request_order[image_ids // IMG_REQ]
    image_perm = jax.random.permutation(key_images, IMGS).astype(jnp.int32)
    img_req = jnp.zeros((IMGS,), jnp.int32).at[image_perm].set(image_owner)
    image_rank = jnp.cumsum(has_images) - 1
    blocks = jnp.arange(NBLK, dtype=jnp.int32)
    slot_ids = jnp.arange(IMG_REQ, dtype=jnp.int32)

    def request_slots(request, allowed):
        clipped = jnp.clip(request, 0, REQS - 1)
        usable = allowed & (has_images[clipped] == 1)
        picked = image_perm[jnp.clip(image_rank[clipped][:, None] * IMG_REQ + slot_ids[None, :], 0, IMGS - 1)]
        return jnp.where(usable[:, None], picked, IMGS)
    block_imgs = jnp.concatenate([request_slots(blocks - 1, blocks >= 1), request_slots(blocks, blocks >= 0)], axis=1)
    return (block_imgs.astype(jnp.int32), img_req, req_start)


def draw_block_imgs(key, part):
    return layout(key)[0]


def draw_img_req(key, part):
    return layout(key)[1]


def draw_req_start(key, part):
    return layout(key)[2]


def draw_queries(key, part):
    own_key = jax.random.fold_in(key, 21)
    noise_key, scale_key = jax.random.split(own_key)
    row_scale = jnp.exp(jax.random.uniform(scale_key, (TOKENS, 1), minval=0.0, maxval=math.log(3.5)))
    rows = jnp.clip(jax.random.normal(noise_key, (TOKENS, H * HD), jnp.float32) * row_scale, -6.0, 6.0)
    return rows.astype(jnp.bfloat16)


def draw_keys(key, part):
    own_key = jax.random.fold_in(key, 31)
    rows = jnp.clip(jax.random.normal(own_key, (IMGS, LAT, H * HD), jnp.float32), -6.0, 6.0)
    return rows.astype(jnp.bfloat16)


def steps_of(key, dims, cuts, least, largest):
    def one(dim, blocks):
        steps = jax.random.uniform(jax.random.fold_in(jax.random.fold_in(key, 6), dim), (blocks,), jnp.float32, least / len(cuts), largest / len(cuts))
        return jnp.repeat(jnp.exp(steps), dims[dim] // blocks).reshape((-1,) + (1,) * (len(dims) - dim - 1))

    level = one(*cuts[0])
    for cut in cuts[1:]:
        level = level * one(*cut)
    return level


def noise(key, extent, deviation, reach, shards=(), kind=jnp.bfloat16):
    entries = deviation * jax.random.normal(key, extent, jnp.float32)
    if shards:
        entries = entries * steps_of(key, extent, shards, -0.22, 0.18)
    return jnp.clip(entries, -reach, reach).astype(kind)


def setup_inputs(seed: int = 0) -> dict:
    seeds = jax.random.split(jax.random.key(seed), 7)
    return {
        "queries": draw_queries(jax.random.fold_in(seeds[6], 71), 0),
        "keys": draw_keys(jax.random.fold_in(seeds[6], 71), 0),
        "values": noise(seeds[2], (IMGS, LAT, H * HD), 1.0, 6.0, ((0, 4), (2, 64))),
        "block_imgs": draw_block_imgs(jax.random.fold_in(seeds[6], 71), 0),
        "img_req": draw_img_req(jax.random.fold_in(seeds[6], 71), 0),
        "req_start": draw_req_start(jax.random.fold_in(seeds[6], 71), 0),
    }


MASKED_SCORE = -1e30


def reference(queries, keys, values, block_imgs, img_req, req_start):
    image_count = keys.shape[0]
    latent_count = keys.shape[1]
    query_blocks = queries.reshape(NBLK, BLOCK, H, HD)

    def attend_block(packed):
        query_block, img_lists, block_index = packed
        safe_ids = jnp.clip(img_lists, 0, image_count - 1)
        key_rows = keys[safe_ids].reshape(MAXVIS * latent_count, H, HD).astype(jnp.float32)
        value_rows = values[safe_ids].reshape(MAXVIS * latent_count, H, HD).astype(jnp.float32)
        position = block_index * BLOCK + jnp.arange(BLOCK, dtype=jnp.int32)
        req_tok = jnp.sum((req_start[None, :] <= position[:, None]).astype(jnp.int32), axis=1).astype(jnp.int32) - 1
        visible = (img_lists < image_count)[None, :] & (img_req[safe_ids][None, :] == req_tok[:, None])
        key_mask = jnp.repeat(visible, latent_count, axis=1)[None]
        scores = jnp.einsum('thd,khd->htk', query_block.astype(jnp.float32), key_rows) * (HD ** -0.5)
        top_score = jnp.max(jnp.where(key_mask, scores, MASKED_SCORE), axis=-1)
        weights = jnp.where(key_mask, jnp.exp(scores - top_score[..., None]), 0.0)
        total_weight = jnp.sum(weights, axis=-1)
        rounded = lax.optimization_barrier(weights.astype(jnp.bfloat16)).astype(jnp.float32)
        numerator = jnp.einsum('htk,khd->thd', rounded, value_rows)
        denom = jnp.where(total_weight > 0, total_weight, 1.0)
        result = numerator / jnp.transpose(denom)[:, :, None]
        return result.astype(jnp.bfloat16).reshape(BLOCK, H * HD)

    outputs = lax.map(attend_block, (query_blocks, block_imgs, jnp.arange(NBLK, dtype=jnp.int32)))
    return outputs.reshape(TOKENS, H * HD)
```

```python
import jax
import jax.numpy as jnp
from jax import lax
from jax.experimental import pallas as pl
from jax.experimental.pallas import tpu as pltpu
from jax.sharding import PartitionSpec as P

HD = 128
BLOCK = 256
GROUP = 4
FAR = 1e30
SCALE2 = HD ** (-0.5) * 1.4426950408889634


def partial_kernel(unroll, lists, owners, starts, q, k, v, out, lse, picked, tops, totals, sums):
    held, lat, _ = k.shape
    images = owners.shape[0]
    requests = starts.shape[0]
    tokens = q.shape[0]
    slots = lists.shape[1] // 2
    first = lax.axis_index("cache") * held
    wide = BLOCK + HD

    def pick(u, r):
        count = jnp.int32(0)
        for s in range(slots):
            picked[u, s] = 0
        for s in range(slots):
            image = lists[r, slots + s]
            local = image - first
            owner = owners[jnp.minimum(image, images - 1)]
            here = (image < images) & (owner == r) & (local >= 0) & (local < held)
            picked[u, count] = jnp.where(here, local, 0)
            count = count + here.astype(jnp.int32)
        return count

    def window(r):
        low = pl.multiple_of(r * BLOCK, BLOCK)
        high = pl.multiple_of(jnp.minimum(low + BLOCK, tokens - HD), HD)
        return jnp.concatenate([q[pl.ds(low, BLOCK), :], q[pl.ds(high, HD), :]], axis=0)

    def chunk(u, r, base, count):
        rows = window(r)
        ids = [picked[u, base + s] for s in range(GROUP)]
        keys = jnp.concatenate([k[i] for i in ids], axis=0)
        scores = lax.dot_general(
            keys, rows, (((1,), (1,)), ((), ())), preferred_element_type=jnp.float32
        )
        parts = [scores[s * lat : (s + 1) * lat] for s in range(GROUP)]
        top = jnp.full((1, wide), -FAR, jnp.float32)
        for s in range(GROUP):
            here = jnp.max(parts[s], axis=0, keepdims=True)
            top = jnp.maximum(top, jnp.where(base + s < count, here, -FAR))
        top = jnp.where(base < count, top, 0.0)
        probs = []
        total = jnp.zeros((1, wide), jnp.float32)
        for s in range(GROUP):
            level = top + jnp.where(base + s < count, 0.0, FAR)
            p = jnp.exp2((parts[s] - level) * SCALE2)
            total = total + jnp.sum(p, axis=0, keepdims=True)
            probs.append(p.astype(jnp.bfloat16))
        vals = jnp.concatenate([v[i] for i in ids], axis=0)
        summed = lax.dot_general(
            vals,
            jnp.concatenate(probs, axis=0),
            (((0,), (0,)), ((), ())),
            preferred_element_type=jnp.float32,
        )
        return top, total, summed

    def step(g, carry):
        counts = []
        for u in range(unroll):
            counts.append(pick(u, g * unroll + u))
        for u in range(unroll):
            tops[u], totals[u], sums[u] = chunk(u, g * unroll + u, 0, counts[u])
        for u in range(unroll):

            @pl.when(counts[u] > GROUP)
            def _():
                top1, total1, sum1 = chunk(u, g * unroll + u, GROUP, counts[u])
                top0 = tops[u]
                both = jnp.maximum(top0, top1)
                scale0 = jnp.exp2((top0 - both) * SCALE2)
                scale1 = jnp.exp2((top1 - both) * SCALE2)
                tops[u] = both
                totals[u] = totals[u] * scale0 + total1 * scale1
                sums[u] = sums[u] * scale0 + sum1 * scale1

        for u in range(unroll):
            r = g * unroll + u
            total = totals[u]
            seen = total > 0
            safe = jnp.where(seen, total, 1.0)
            level = jnp.where(seen, tops[u] * SCALE2 + jnp.log2(safe), -FAR)
            result = (sums[u] * (1.0 / safe)).astype(jnp.bfloat16)
            low = pl.multiple_of(r * BLOCK, BLOCK)
            position = low + lax.broadcasted_iota(jnp.int32, (1, HD), 1)
            mine = position >= starts[r]
            lse[:, pl.ds(low, HD)] = jnp.where(mine, level[:, :HD], lse[:, pl.ds(low, HD)])
            old = out[:, pl.ds(low, HD)].astype(jnp.float32)
            new = result[:, :HD].astype(jnp.float32)
            out[:, pl.ds(low, HD)] = jnp.where(mine, new, old).astype(jnp.bfloat16)
            mid = pl.multiple_of(low + HD, HD)
            lse[:, pl.ds(mid, HD)] = level[:, HD:BLOCK]
            out[:, pl.ds(mid, HD)] = result[:, HD:BLOCK]

            @pl.when(r < requests - 1)
            def _():
                high = pl.multiple_of(low + BLOCK, HD)
                lse[:, pl.ds(high, HD)] = level[:, BLOCK:]
                out[:, pl.ds(high, HD)] = result[:, BLOCK:]

        return carry

    lax.fori_loop(0, requests // unroll, step, 0)


def partial_attention(q, k, v, block_imgs, img_req, req_start):
    tokens = q.shape[0]
    unroll = 2
    wide = BLOCK + HD
    smem = pl.BlockSpec(memory_space=pltpu.SMEM)
    vmem = pl.BlockSpec(memory_space=pltpu.VMEM)

    def kernel(*refs):
        partial_kernel(unroll, *refs)

    return pl.pallas_call(
        kernel,
        out_shape=(
            jax.ShapeDtypeStruct((HD, tokens), jnp.bfloat16),
            jax.ShapeDtypeStruct((1, tokens), jnp.float32),
        ),
        in_specs=[smem, smem, smem, vmem, vmem, vmem],
        out_specs=(vmem, vmem),
        scratch_shapes=[
            pltpu.SMEM((unroll, 16), jnp.int32),
            pltpu.VMEM((unroll, 1, wide), jnp.float32),
            pltpu.VMEM((unroll, 1, wide), jnp.float32),
            pltpu.VMEM((unroll, HD, wide), jnp.float32),
        ],
        name="partial",
    )(block_imgs, img_req, req_start, q, k, v)


def shards(queries, keys, values, block_imgs, img_req, req_start):
    ctx = lax.axis_size("ctx")
    cache = lax.axis_size("cache")
    me = lax.axis_index("cache")
    rows = queries.shape[0]
    part = rows // cache
    tokens = rows * ctx
    quarter = lax.dynamic_slice_in_dim(queries, me * part, part, 0)
    spread = lax.all_to_all(quarter, "ctx", split_axis=1, concat_axis=0, tiled=True)
    gathered = lax.all_gather(spread.reshape(ctx, part, HD), "cache")
    q = jnp.transpose(gathered, (1, 0, 2, 3)).reshape(tokens, HD)
    out, lse = partial_attention(q, keys, values, block_imgs, img_req, req_start)
    deep = HD // cache
    parts = lax.all_to_all(out.reshape(cache, deep, tokens), "cache", 0, 0)
    levels = lax.all_gather(lse, "cache")
    top = jnp.max(levels, axis=0)
    weights = jnp.exp2(levels - top)
    merged = jnp.sum(parts.astype(jnp.float32) * weights, axis=0) / jnp.sum(weights, axis=0)
    merged = merged.astype(jnp.bfloat16)
    mine = lax.all_to_all(
        jnp.transpose(merged.reshape(deep, ctx, rows), (1, 0, 2)), "ctx", 0, 0
    )
    every = lax.all_gather(mine, "cache")
    return jnp.transpose(every, (3, 1, 0, 2)).reshape(rows, ctx * HD)


def solution(mesh):
    placed = (P("ctx", None), P("cache", None, "ctx"), P("cache", None, "ctx"), P(), P(), P())
    return jax.shard_map(
        shards, mesh=mesh, in_specs=placed, out_specs=P("ctx", None), check_vma=False
    )
```

```python
import jax
import jax.numpy as jnp
from jax import lax
from jax.experimental import pallas as pl
from jax.experimental.pallas import tpu as pltpu
from jax.sharding import PartitionSpec as P

HD = 128
BLOCK = 256
GROUP = 4
FAR = 1e30
SCALE2 = HD ** (-0.5) * 1.4426950408889634


def partial_kernel(unroll, lists, owners, starts, q, k, v, out, lse, picked, tops, totals, sums):
    held, lat, _ = k.shape
    images = owners.shape[0]
    requests = starts.shape[0]
    tokens = q.shape[0]
    slots = lists.shape[1] // 2
    first = lax.axis_index("cache") * held
    wide = BLOCK + HD

    def pick(u, r):
        count = jnp.int32(0)
        for s in range(slots):
            picked[u, s] = 0
        for s in range(slots):
            image = lists[r, slots + s]
            local = image - first
            owner = owners[jnp.minimum(image, images - 1)]
            here = (image < images) & (owner == r) & (local >= 0) & (local < held)
            picked[u, count] = jnp.where(here, local, 0)
            count = count + here.astype(jnp.int32)
        return count

    def window(r):
        low = pl.multiple_of(r * BLOCK, BLOCK)
        high = pl.multiple_of(jnp.minimum(low + BLOCK, tokens - HD), HD)
        return jnp.concatenate([q[pl.ds(low, BLOCK), :], q[pl.ds(high, HD), :]], axis=0)

    def chunk(u, r, base, count):
        rows = window(r)
        ids = [picked[u, base + s] for s in range(GROUP)]
        keys = jnp.concatenate([k[i] for i in ids], axis=0)
        scores = lax.dot_general(
            keys, rows, (((1,), (1,)), ((), ())), preferred_element_type=jnp.float32
        )
        parts = [scores[s * lat : (s + 1) * lat] for s in range(GROUP)]
        top = jnp.full((1, wide), -FAR, jnp.float32)
        for s in range(GROUP):
            here = jnp.max(parts[s], axis=0, keepdims=True)
            top = jnp.maximum(top, jnp.where(base + s < count, here, -FAR))
        top = jnp.where(base < count, top, 0.0)
        probs = []
        total = jnp.zeros((1, wide), jnp.float32)
        for s in range(GROUP):
            level = top + jnp.where(base + s < count, 0.0, FAR)
            p = jnp.exp2((parts[s] - level) * SCALE2)
            total = total + jnp.sum(p, axis=0, keepdims=True)
            probs.append(p.astype(jnp.bfloat16))
        vals = jnp.concatenate([v[i] for i in ids], axis=0)
        summed = lax.dot_general(
            vals,
            jnp.concatenate(probs, axis=0),
            (((0,), (0,)), ((), ())),
            preferred_element_type=jnp.float32,
        )
        return top, total, summed

    def step(g, carry):
        counts = []
        for u in range(unroll):
            counts.append(pick(u, g * unroll + u))
        for u in range(unroll):
            tops[u], totals[u], sums[u] = chunk(u, g * unroll + u, 0, counts[u])
        for u in range(unroll):

            @pl.when(counts[u] > GROUP)
            def _():
                top1, total1, sum1 = chunk(u, g * unroll + u, GROUP, counts[u])
                top0 = tops[u]
                both = jnp.maximum(top0, top1)
                scale0 = jnp.exp2((top0 - both) * SCALE2)
                scale1 = jnp.exp2((top1 - both) * SCALE2)
                tops[u] = both
                totals[u] = totals[u] * scale0 + total1 * scale1
                sums[u] = sums[u] * scale0 + sum1 * scale1

        for u in range(unroll):
            r = g * unroll + u
            total = totals[u]
            seen = total > 0
            safe = jnp.where(seen, total, 1.0)
            level = jnp.where(seen, tops[u] * SCALE2 + jnp.log2(safe), -FAR)
            result = (sums[u] * (1.0 / safe)).astype(jnp.bfloat16)
            low = pl.multiple_of(r * BLOCK, BLOCK)
            position = low + lax.broadcasted_iota(jnp.int32, (1, HD), 1)
            mine = position >= starts[r]
            lse[:, pl.ds(low, HD)] = jnp.where(mine, level[:, :HD], lse[:, pl.ds(low, HD)])
            old = out[:, pl.ds(low, HD)].astype(jnp.float32)
            new = result[:, :HD].astype(jnp.float32)
            out[:, pl.ds(low, HD)] = jnp.where(mine, new, old).astype(jnp.bfloat16)
            mid = pl.multiple_of(low + HD, HD)
            lse[:, pl.ds(mid, HD)] = level[:, HD:BLOCK]
            out[:, pl.ds(mid, HD)] = result[:, HD:BLOCK]

            @pl.when(r < requests - 1)
            def _():
                high = pl.multiple_of(low + BLOCK, HD)
                lse[:, pl.ds(high, HD)] = level[:, BLOCK:]
                out[:, pl.ds(high, HD)] = result[:, BLOCK:]

        return carry

    lax.fori_loop(0, requests // unroll, step, 0)


def partial_attention(q, k, v, block_imgs, img_req, req_start):
    tokens = q.shape[0]
    unroll = 2
    wide = BLOCK + HD
    smem = pl.BlockSpec(memory_space=pltpu.SMEM)
    vmem = pl.BlockSpec(memory_space=pltpu.VMEM)

    def kernel(*refs):
        partial_kernel(unroll, *refs)

    return pl.pallas_call(
        kernel,
        out_shape=(
            jax.ShapeDtypeStruct((HD, tokens), jnp.bfloat16),
            jax.ShapeDtypeStruct((1, tokens), jnp.float32),
        ),
        in_specs=[smem, smem, smem, vmem, vmem, vmem],
        out_specs=(vmem, vmem),
        scratch_shapes=[
            pltpu.SMEM((unroll, 16), jnp.int32),
            pltpu.VMEM((unroll, 1, wide), jnp.float32),
            pltpu.VMEM((unroll, 1, wide), jnp.float32),
            pltpu.VMEM((unroll, HD, wide), jnp.float32),
        ],
        name="partial",
    )(block_imgs, img_req, req_start, q, k, v)


NX = 4
NZ = 8
MESH = pl.DeviceIdType.MESH


def push(src, dst, sent, landed, ctx, cache):
    return pltpu.make_async_remote_copy(
        src_ref=src,
        dst_ref=dst,
        send_sem=sent,
        recv_sem=landed,
        device_id=(ctx, cache),
        device_id_type=MESH,
    )


def turn(i):
    return 0 if i == 0 else ((i + 1) // 2 if i % 2 else NZ - i // 2)


def place():
    c = lax.axis_index("ctx")
    y = lax.axis_index("cache")
    return c, y, c // (2 * NZ), lax.rem(c // 2, NZ), lax.rem(c, 2)


def greet(c, y, offsets):
    barrier = pltpu.get_barrier_semaphore()

    def ring(s, carry):
        pl.semaphore_signal(
            barrier, inc=1, device_id=(lax.rem(c + s, 2 * NX * NZ), y), device_id_type=MESH
        )
        return carry

    lax.fori_loop(1, 2 * NX * NZ, ring, 0)
    for o in offsets:
        pl.semaphore_signal(
            barrier, inc=1, device_id=(c, lax.rem(y + o, 4)), device_id_type=MESH
        )
    pl.semaphore_wait(barrier, 2 * NX * NZ - 1 + len(offsets))


def share(buf, sems, c, y, z, part):
    sent, came, left, right, far = sems
    up = lax.rem(y + 1, 4)
    down = lax.rem(y + 3, 4)

    def piece(dz, who):
        return buf.at[:, lax.rem(z + NZ - dz, NZ), :, pl.ds(who * part, part), :]

    def forward(i):
        dz = turn(i)
        own = piece(dz, y)
        push(own, own, sent.at[0, dz], came.at[dz], c, up).wait_recv()
        push(own, own, sent.at[0, dz], left.at[dz], c, up).start()
        push(own, own, sent.at[1, dz], right.at[dz], c, down).start()

    def relay(i):
        dz = turn(i)
        if i % 2 == 0:
            got = piece(dz, down)
            push(got, got, sent.at[2, dz], left.at[dz], c, up).wait_recv()
            push(got, got, sent.at[2, dz], far.at[dz], c, up).start()
        else:
            got = piece(dz, up)
            push(got, got, sent.at[2, dz], right.at[dz], c, down).wait_recv()
            push(got, got, sent.at[2, dz], far.at[dz], c, down).start()

    def finish(i):
        dz = turn(i)
        if i % 2 == 0:
            got = piece(dz, up)
            push(got, got, sent.at[2, dz], right.at[dz], c, down).wait_recv()
        else:
            got = piece(dz, down)
            push(got, got, sent.at[2, dz], left.at[dz], c, up).wait_recv()
        got = piece(dz, lax.rem(y + 2, 4))
        push(got, got, sent.at[2, dz], far.at[dz], c, up).wait_recv()
        own = piece(dz, y)
        for k in range(3):
            push(own, own, sent.at[k, dz], far.at[dz], c, up).wait_send()

    return forward, relay, finish


def spread_kernel(part, q, buf, out_sem, sent, came, left, right, far):
    c, y, x, z, core = place()
    greet(c, y, (1, 3))
    rows = pl.ds(y * part, part)
    mine = buf.at[x, z, core, rows, :]

    def block(to):
        return q.at[rows, pl.ds(pl.multiple_of(to * HD, HD), HD)]

    for i in range(NZ):
        dz = turn(i)

        def send(j, carry):
            to = (
                lax.rem(x + j // 2, NX) * (2 * NZ)
                + lax.rem(z + dz, NZ) * 2
                + lax.rem(core + lax.rem(j, 2), 2)
            )
            push(block(to), mine, out_sem.at[dz], came.at[dz], to, y).start()
            return carry

        if i == 0:
            pltpu.make_async_copy(block(c), mine, came.at[0]).start()
        lax.fori_loop(1 if i == 0 else 0, 2 * NX, send, 0)
    forward, relay, finish = share(buf, (sent, came, left, right, far), c, y, z, part)
    for i in range(NZ + 1):
        if i < NZ:
            forward(i)
        if i >= 1:
            relay(i - 1)
    for i in range(NZ):
        dz = turn(i)
        finish(i)
        whole = buf.at[:, z, :, rows, :]
        if i == 0:
            some = q.at[rows, pl.ds(0, (2 * NX - 1) * HD)]
            push(some, some, out_sem.at[dz], came.at[dz], c, y).wait_send()
        else:
            push(whole, whole, out_sem.at[dz], came.at[dz], c, y).wait_send()


def spread(queries, part):
    def kernel(*refs):
        spread_kernel(part, *refs)

    dma = pltpu.SemaphoreType.DMA
    return pl.pallas_call(
        kernel,
        out_shape=jax.ShapeDtypeStruct((NX, NZ, 2, 4 * part, HD), jnp.bfloat16),
        in_specs=[pl.BlockSpec(memory_space=pl.ANY)],
        out_specs=pl.BlockSpec(memory_space=pltpu.VMEM),
        scratch_shapes=[dma((NZ,)), dma((3, NZ)), dma((NZ,)), dma((NZ,)), dma((NZ,)), dma((NZ,))],
        compiler_params=pltpu.CompilerParams(collective_id=1, has_side_effects=True),
        name="spread",
    )(queries)


def shards(queries, keys, values, block_imgs, img_req, req_start):
    ctx = lax.axis_size("ctx")
    cache = lax.axis_size("cache")
    rows = queries.shape[0]
    part = rows // cache
    tokens = rows * ctx
    q = spread(queries, part).reshape(tokens, HD)
    out, lse = partial_attention(q, keys, values, block_imgs, img_req, req_start)
    deep = HD // cache
    parts = lax.all_to_all(out.reshape(cache, deep, tokens), "cache", 0, 0)
    levels = lax.all_gather(lse, "cache")
    top = jnp.max(levels, axis=0)
    weights = jnp.exp2(levels - top)
    merged = jnp.sum(parts.astype(jnp.float32) * weights, axis=0) / jnp.sum(weights, axis=0)
    merged = merged.astype(jnp.bfloat16)
    mine = lax.all_to_all(
        jnp.transpose(merged.reshape(deep, ctx, rows), (1, 0, 2)), "ctx", 0, 0
    )
    every = lax.all_gather(mine, "cache")
    return jnp.transpose(every, (3, 1, 0, 2)).reshape(rows, ctx * HD)


def solution(mesh):
    placed = (P("ctx", None), P("cache", None, "ctx"), P("cache", None, "ctx"), P(), P(), P())
    return jax.shard_map(
        shards, mesh=mesh, in_specs=placed, out_specs=P("ctx", None), check_vma=False
    )
```

```python
import jax
import jax.numpy as jnp
from jax import lax
from jax.experimental import pallas as pl
from jax.experimental.pallas import tpu as pltpu
from jax.sharding import PartitionSpec as P

HD = 128
BLOCK = 256
GROUP = 4
FAR = 1e30
SCALE2 = HD ** (-0.5) * 1.4426950408889634


def partial_kernel(unroll, lists, owners, starts, q, k, v, out, lse, picked, tops, totals, sums):
    held, lat, _ = k.shape
    images = owners.shape[0]
    requests = starts.shape[0]
    tokens = q.shape[0]
    slots = lists.shape[1] // 2
    first = lax.axis_index("cache") * held
    wide = BLOCK + HD

    def pick(u, r):
        count = jnp.int32(0)
        for s in range(slots):
            picked[u, s] = 0
        for s in range(slots):
            image = lists[r, slots + s]
            local = image - first
            owner = owners[jnp.minimum(image, images - 1)]
            here = (image < images) & (owner == r) & (local >= 0) & (local < held)
            picked[u, count] = jnp.where(here, local, 0)
            count = count + here.astype(jnp.int32)
        return count

    def window(r):
        low = pl.multiple_of(r * BLOCK, BLOCK)
        high = pl.multiple_of(jnp.minimum(low + BLOCK, tokens - HD), HD)
        return jnp.concatenate([q[pl.ds(low, BLOCK), :], q[pl.ds(high, HD), :]], axis=0)

    def chunk(u, r, base, count):
        rows = window(r)
        ids = [picked[u, base + s] for s in range(GROUP)]
        keys = jnp.concatenate([k[i] for i in ids], axis=0)
        scores = lax.dot_general(
            keys, rows, (((1,), (1,)), ((), ())), preferred_element_type=jnp.float32
        )
        parts = [scores[s * lat : (s + 1) * lat] for s in range(GROUP)]
        top = jnp.full((1, wide), -FAR, jnp.float32)
        for s in range(GROUP):
            here = jnp.max(parts[s], axis=0, keepdims=True)
            top = jnp.maximum(top, jnp.where(base + s < count, here, -FAR))
        top = jnp.where(base < count, top, 0.0)
        probs = []
        total = jnp.zeros((1, wide), jnp.float32)
        for s in range(GROUP):
            level = top + jnp.where(base + s < count, 0.0, FAR)
            p = jnp.exp2((parts[s] - level) * SCALE2)
            total = total + jnp.sum(p, axis=0, keepdims=True)
            probs.append(p.astype(jnp.bfloat16))
        vals = jnp.concatenate([v[i] for i in ids], axis=0)
        summed = lax.dot_general(
            vals,
            jnp.concatenate(probs, axis=0),
            (((0,), (0,)), ((), ())),
            preferred_element_type=jnp.float32,
        )
        return top, total, summed

    def step(g, carry):
        counts = []
        for u in range(unroll):
            counts.append(pick(u, g * unroll + u))
        for u in range(unroll):
            tops[u], totals[u], sums[u] = chunk(u, g * unroll + u, 0, counts[u])
        for u in range(unroll):

            @pl.when(counts[u] > GROUP)
            def _():
                top1, total1, sum1 = chunk(u, g * unroll + u, GROUP, counts[u])
                top0 = tops[u]
                both = jnp.maximum(top0, top1)
                scale0 = jnp.exp2((top0 - both) * SCALE2)
                scale1 = jnp.exp2((top1 - both) * SCALE2)
                tops[u] = both
                totals[u] = totals[u] * scale0 + total1 * scale1
                sums[u] = sums[u] * scale0 + sum1 * scale1

        for u in range(unroll):
            r = g * unroll + u
            total = totals[u]
            seen = total > 0
            safe = jnp.where(seen, total, 1.0)
            level = jnp.where(seen, tops[u] * SCALE2 + jnp.log2(safe), -FAR)
            result = (sums[u] * (1.0 / safe)).astype(jnp.bfloat16)
            position = r * BLOCK + lax.broadcasted_iota(jnp.int32, (1, HD), 1)
            mine = position >= starts[r]
            lse[r, :, :HD] = jnp.where(mine, level[:, :HD], lse[r, :, :HD])
            old = out[r, :, :HD].astype(jnp.float32)
            new = result[:, :HD].astype(jnp.float32)
            out[r, :, :HD] = jnp.where(mine, new, old).astype(jnp.bfloat16)
            lse[r, :, HD:] = level[:, HD:BLOCK]
            out[r, :, HD:] = result[:, HD:BLOCK]

            @pl.when(r < requests - 1)
            def _():
                lse[r + 1, :, :HD] = level[:, BLOCK:]
                out[r + 1, :, :HD] = result[:, BLOCK:]

        return carry

    lax.fori_loop(0, requests // unroll, step, 0)


def partial_attention(q, k, v, block_imgs, img_req, req_start):
    tokens = q.shape[0]
    unroll = 2
    wide = BLOCK + HD
    smem = pl.BlockSpec(memory_space=pltpu.SMEM)
    vmem = pl.BlockSpec(memory_space=pltpu.VMEM)

    def kernel(*refs):
        partial_kernel(unroll, *refs)

    return pl.pallas_call(
        kernel,
        out_shape=(
            jax.ShapeDtypeStruct((tokens // BLOCK, HD, BLOCK), jnp.bfloat16),
            jax.ShapeDtypeStruct((tokens // BLOCK, 1, BLOCK), jnp.float32),
        ),
        in_specs=[smem, smem, smem, vmem, vmem, vmem],
        out_specs=(vmem, vmem),
        scratch_shapes=[
            pltpu.SMEM((unroll, 16), jnp.int32),
            pltpu.VMEM((unroll, 1, wide), jnp.float32),
            pltpu.VMEM((unroll, 1, wide), jnp.float32),
            pltpu.VMEM((unroll, HD, wide), jnp.float32),
        ],
        name="partial",
    )(block_imgs, img_req, req_start, q, k, v)


NX = 4
NZ = 8
MESH = pl.DeviceIdType.MESH


def push(src, dst, sent, landed, ctx, cache):
    return pltpu.make_async_remote_copy(
        src_ref=src,
        dst_ref=dst,
        send_sem=sent,
        recv_sem=landed,
        device_id=(ctx, cache),
        device_id_type=MESH,
    )


def turn(i):
    return 0 if i == 0 else ((i + 1) // 2 if i % 2 else NZ - i // 2)


def place():
    c = lax.axis_index("ctx")
    y = lax.axis_index("cache")
    return c, y, c // (2 * NZ), lax.rem(c // 2, NZ), lax.rem(c, 2)


def greet(c, y, offsets):
    barrier = pltpu.get_barrier_semaphore()

    def ring(s, carry):
        pl.semaphore_signal(
            barrier, inc=1, device_id=(lax.rem(c + s, 2 * NX * NZ), y), device_id_type=MESH
        )
        return carry

    lax.fori_loop(1, 2 * NX * NZ, ring, 0)
    for o in offsets:
        pl.semaphore_signal(
            barrier, inc=1, device_id=(c, lax.rem(y + o, 4)), device_id_type=MESH
        )
    pl.semaphore_wait(barrier, 2 * NX * NZ - 1 + len(offsets))


def share(buf, sems, c, y, z, part):
    sent, came, left, right, far = sems
    up = lax.rem(y + 1, 4)
    down = lax.rem(y + 3, 4)

    def piece(dz, who):
        return buf.at[:, lax.rem(z + NZ - dz, NZ), :, pl.ds(who * part, part), :]

    def forward(i):
        dz = turn(i)
        own = piece(dz, y)
        push(own, own, sent.at[0, dz], came.at[dz], c, up).wait_recv()
        push(own, own, sent.at[0, dz], left.at[dz], c, up).start()
        push(own, own, sent.at[1, dz], right.at[dz], c, down).start()

    def relay(i):
        dz = turn(i)
        if i % 2 == 0:
            got = piece(dz, down)
            push(got, got, sent.at[2, dz], left.at[dz], c, up).wait_recv()
            push(got, got, sent.at[2, dz], far.at[dz], c, up).start()
        else:
            got = piece(dz, up)
            push(got, got, sent.at[2, dz], right.at[dz], c, down).wait_recv()
            push(got, got, sent.at[2, dz], far.at[dz], c, down).start()

    def finish(i):
        dz = turn(i)
        if i % 2 == 0:
            got = piece(dz, up)
            push(got, got, sent.at[2, dz], right.at[dz], c, down).wait_recv()
        else:
            got = piece(dz, down)
            push(got, got, sent.at[2, dz], left.at[dz], c, up).wait_recv()
        got = piece(dz, lax.rem(y + 2, 4))
        push(got, got, sent.at[2, dz], far.at[dz], c, up).wait_recv()
        own = piece(dz, y)
        for k in range(3):
            push(own, own, sent.at[k, dz], far.at[dz], c, up).wait_send()

    return forward, relay, finish


def spread_kernel(part, q, buf, out_sem, sent, came, left, right, far):
    c, y, x, z, core = place()
    greet(c, y, (1, 3))
    rows = pl.ds(y * part, part)
    mine = buf.at[x, z, core, rows, :]

    def block(to):
        return q.at[rows, pl.ds(pl.multiple_of(to * HD, HD), HD)]

    for i in range(NZ):
        dz = turn(i)

        def send(j, carry):
            to = (
                lax.rem(x + j // 2, NX) * (2 * NZ)
                + lax.rem(z + dz, NZ) * 2
                + lax.rem(core + lax.rem(j, 2), 2)
            )
            push(block(to), mine, out_sem.at[dz], came.at[dz], to, y).start()
            return carry

        if i == 0:
            pltpu.make_async_copy(block(c), mine, came.at[0]).start()
        lax.fori_loop(1 if i == 0 else 0, 2 * NX, send, 0)
    forward, relay, finish = share(buf, (sent, came, left, right, far), c, y, z, part)
    for i in range(NZ + 1):
        if i < NZ:
            forward(i)
        if i >= 1:
            relay(i - 1)
    for i in range(NZ):
        dz = turn(i)
        finish(i)
        whole = buf.at[:, z, :, rows, :]
        if i == 0:
            some = q.at[rows, pl.ds(0, (2 * NX - 1) * HD)]
            push(some, some, out_sem.at[dz], came.at[dz], c, y).wait_send()
        else:
            push(whole, whole, out_sem.at[dz], came.at[dz], c, y).wait_send()


def spread(queries, part):
    def kernel(*refs):
        spread_kernel(part, *refs)

    dma = pltpu.SemaphoreType.DMA
    return pl.pallas_call(
        kernel,
        out_shape=jax.ShapeDtypeStruct((NX, NZ, 2, 4 * part, HD), jnp.bfloat16),
        in_specs=[pl.BlockSpec(memory_space=pl.ANY)],
        out_specs=pl.BlockSpec(memory_space=pltpu.VMEM),
        scratch_shapes=[dma((NZ,)), dma((3, NZ)), dma((NZ,)), dma((NZ,)), dma((NZ,)), dma((NZ,))],
        compiler_params=pltpu.CompilerParams(collective_id=1, has_side_effects=True),
        name="spread",
    )(queries)


def merge_kernel(
    deep, part, lse, buf, levels, alpha, relayed, raw, added, adding, final,
    lse_sent, lse_came, a_sent, a_came, r_sent, r_came, m_sent, m_came,
    out_sem, came, sent, left, right, far,
):
    c, y, x, z, core = place()
    up = lax.rem(y + 1, 4)
    down = lax.rem(y + 3, 4)
    across = lax.rem(y + 2, 4)
    greet(c, y, (1, 2, 3))

    def rows(who):
        return pl.ds(pl.multiple_of(who * deep, deep), deep)

    def chip(i):
        return lax.rem(z + turn(i), NZ)

    own_lse = pltpu.make_async_copy(lse, levels.at[y], lse_came.at[3])
    own_lse.start()
    tell = [
        push(lse, levels.at[y], lse_sent.at[o - 1], lse_came.at[o - 1], c, lax.rem(y + o, 4))
        for o in (1, 2, 3)
    ]
    for t in tell:
        t.start()

    def offers(i):
        zs = chip(i)
        return (
            push(part.at[pl.ds(0, 2), zs, rows(across), :], relayed.at[0, i],
                 a_sent.at[0, i], a_came.at[0, i], c, up),
            push(part.at[pl.ds(2, 2), zs, rows(across), :], relayed.at[1, i],
                 a_sent.at[1, i], a_came.at[1, i], c, down),
            push(part.at[pl.ds(2, 2), zs, rows(up), :], raw.at[0, i],
                 r_sent.at[0, i], r_came.at[0, i], c, up),
            push(part.at[pl.ds(0, 2), zs, rows(down), :], raw.at[1, i],
                 r_sent.at[1, i], r_came.at[1, i], c, down),
        )

    offered = [offers(i) for i in range(NZ)]

    def offer(i):
        for p in offered[i]:
            p.start()

    def adds(i):
        return (
            push(adding.at[0, i], added.at[0, i], m_sent.at[0, i], m_came.at[0, i], c, up),
            push(adding.at[1, i], added.at[1, i], m_sent.at[1, i], m_came.at[1, i], c, down),
        )

    added_to = [adds(i) for i in range(NZ)]

    def weigh(who, k, zs, block):
        return block.astype(jnp.float32) * alpha[who, k * NZ + zs]

    def add(i):
        zs = chip(i)
        ready = offered[i]
        ready[0].wait_recv()
        ready[1].wait_recv()
        for k in range(2):
            adding[0, i, k] = (
                weigh(down, k, zs, relayed[0, i, k]) + weigh(y, k, zs, part[k, zs, rows(up), :])
            ).astype(jnp.bfloat16)
            adding[1, i, k] = (
                weigh(up, k + 2, zs, relayed[1, i, k])
                + weigh(y, k + 2, zs, part[k + 2, zs, rows(down), :])
            ).astype(jnp.bfloat16)

    def complete(i):
        zs = chip(i)
        ready = offered[i]
        ready[2].wait_recv()
        ready[3].wait_recv()
        for p in added_to[i]:
            p.wait_recv()
        for k in range(2):
            final[i, k] = (
                weigh(y, k, zs, part[k, zs, rows(y), :])
                + added[0, i, k].astype(jnp.float32)
                + weigh(up, k, zs, raw[1, i, k])
            ).astype(jnp.bfloat16)
            final[i, k + 2] = (
                weigh(y, k + 2, zs, part[k + 2, zs, rows(y), :])
                + added[1, i, k].astype(jnp.float32)
                + weigh(down, k + 2, zs, raw[0, i, k])
            ).astype(jnp.bfloat16)

    mine = buf.at[x, z, core, pl.ds(y * deep, deep), :]

    def scatter(i):
        dz = turn(i)
        zs = chip(i)

        def block(to_x, to_core):
            return final.at[i, to_x, :, pl.ds(pl.multiple_of(to_core * HD, HD), HD)]

        def send(j, carry):
            to_x = lax.rem(x + j // 2, NX)
            to_core = lax.rem(core + lax.rem(j, 2), 2)
            to = to_x * (2 * NZ) + zs * 2 + to_core
            push(block(to_x, to_core), mine, out_sem.at[dz], came.at[dz], to, y).start()
            return carry

        if i == 0:
            pltpu.make_async_copy(block(x, core), mine, came.at[0]).start()
        lax.fori_loop(1 if i == 0 else 0, 2 * NX, send, 0)

    forward, relay, finish = share(buf, (sent, came, left, right, far), c, y, z, deep)
    offer(0)
    offer(1)
    own_lse.wait()
    for t in tell:
        t.wait_recv()
    tops = jnp.maximum(
        jnp.maximum(levels[0], levels[1]), jnp.maximum(levels[2], levels[3])
    )
    weights = [jnp.exp2(levels[k] - tops) for k in range(4)]
    scale = 1.0 / (weights[0] + weights[1] + weights[2] + weights[3])
    for k in range(4):
        alpha[k] = weights[k] * scale
    for t in range(NZ + 3):
        if t + 2 < NZ:
            offer(t + 2)
        if t < NZ:
            add(t)
        if 0 <= t - 1 < NZ:
            complete(t - 1)
        if t < NZ:
            for p in added_to[t]:
                p.start()
        if 0 <= t - 1 < NZ:
            scatter(t - 1)
        if 0 <= t - 2 < NZ:
            forward(t - 2)
        if 0 <= t - 3 < NZ:
            relay(t - 3)
    for i in range(NZ):
        dz = turn(i)
        finish(i)
        for p in offered[i] + added_to[i]:
            p.wait_send()
        if i == 0:
            some = buf.at[0, pl.ds(0, 2 * NX - 1), 0, pl.ds(0, deep), :]
            push(some, some, out_sem.at[dz], came.at[dz], c, y).wait_send()
        else:
            push(final.at[i], final.at[i], out_sem.at[dz], came.at[dz], c, y).wait_send()
    for t in tell:
        t.wait_send()


def merge(parts, lse, deep):
    def kernel(*refs):
        merge_kernel(deep, *refs)

    dma = pltpu.SemaphoreType.DMA
    vmem = pl.BlockSpec(memory_space=pltpu.VMEM)
    half = (2, NZ, 2, deep, BLOCK)
    return pl.pallas_call(
        kernel,
        out_shape=jax.ShapeDtypeStruct((NX, NZ, 2, HD, HD), jnp.bfloat16),
        in_specs=[vmem, vmem],
        out_specs=vmem,
        scratch_shapes=[
            pltpu.VMEM((4, NX * NZ, 1, BLOCK), jnp.float32),
            pltpu.VMEM((4, NX * NZ, 1, BLOCK), jnp.float32),
            pltpu.VMEM(half, jnp.bfloat16),
            pltpu.VMEM(half, jnp.bfloat16),
            pltpu.VMEM(half, jnp.bfloat16),
            pltpu.VMEM(half, jnp.bfloat16),
            pltpu.VMEM((NZ, NX, deep, BLOCK), jnp.bfloat16),
            dma((3,)), dma((4,)),
            dma((2, NZ)), dma((2, NZ)), dma((2, NZ)), dma((2, NZ)), dma((2, NZ)), dma((2, NZ)),
            dma((NZ,)), dma((NZ,)), dma((3, NZ)), dma((NZ,)), dma((NZ,)), dma((NZ,)),
        ],
        compiler_params=pltpu.CompilerParams(collective_id=2, has_side_effects=True),
        name="merge",
    )(parts, lse)


def turn_kernel(src, dst):
    for k in range(src.shape[0]):
        dst[:, k * HD : (k + 1) * HD] = src[k].T


def turned(heads):
    count, _, rows = heads.shape
    step = 8
    return pl.pallas_call(
        turn_kernel,
        grid=(count // step,),
        out_shape=jax.ShapeDtypeStruct((rows, count * HD), heads.dtype),
        in_specs=[pl.BlockSpec((step, HD, rows), lambda i: (i, 0, 0))],
        out_specs=pl.BlockSpec((rows, step * HD), lambda i: (0, i)),
        name="turned",
    )(heads)


def shards(queries, keys, values, block_imgs, img_req, req_start):
    ctx = lax.axis_size("ctx")
    cache = lax.axis_size("cache")
    rows = queries.shape[0]
    part = rows // cache
    tokens = rows * ctx
    q = spread(queries, part).reshape(tokens, HD)
    out, lse = partial_attention(q, keys, values, block_imgs, img_req, req_start)
    deep = HD // cache
    heads = merge(out.reshape(NX, NZ, HD, BLOCK), lse, deep)
    return turned(heads.reshape(ctx, HD, rows))


def solution(mesh):
    placed = (P("ctx", None), P("cache", None, "ctx"), P("cache", None, "ctx"), P(), P(), P())
    return jax.shard_map(
        shards, mesh=mesh, in_specs=placed, out_specs=P("ctx", None), check_vma=False
    )
```

```python
import jax
import jax.numpy as jnp
from jax import lax
from jax.experimental import pallas as pl
from jax.experimental.pallas import tpu as pltpu
from jax.sharding import PartitionSpec as P

HD = 128
BLOCK = 256
GROUP = 4
FAR = 1e30
SCALE2 = HD ** (-0.5) * 1.4426950408889634


def partial_kernel(unroll, lists, owners, starts, q, k, v, out, lse, picked, tops, totals, sums):
    held, lat, _ = k.shape
    images = owners.shape[0]
    requests = starts.shape[0]
    tokens = q.shape[0]
    slots = lists.shape[0] // 2
    first = lax.axis_index("cache") * held
    wide = BLOCK + HD

    def pick(u, r):
        count = jnp.int32(0)
        for s in range(slots):
            picked[u, s] = 0
        for s in range(slots):
            image = lists[slots + s, r]
            local = image - first
            owner = owners[jnp.minimum(image, images - 1)]
            here = (image < images) & (owner == r) & (local >= 0) & (local < held)
            picked[u, count] = jnp.where(here, local, 0)
            count = count + here.astype(jnp.int32)
        return count

    def window(r):
        low = pl.multiple_of(r * BLOCK, BLOCK)
        high = pl.multiple_of(jnp.minimum(low + BLOCK, tokens - HD), HD)
        return jnp.concatenate([q[pl.ds(low, BLOCK), :], q[pl.ds(high, HD), :]], axis=0)

    def chunk(u, r, base, count):
        rows = window(r)
        ids = [picked[u, base + s] for s in range(GROUP)]
        keys = jnp.concatenate([k[i] for i in ids], axis=0)
        scores = lax.dot_general(
            keys, rows, (((1,), (1,)), ((), ())), preferred_element_type=jnp.float32
        )
        parts = [scores[s * lat : (s + 1) * lat] for s in range(GROUP)]
        top = jnp.full((1, wide), -FAR, jnp.float32)
        for s in range(GROUP):
            here = jnp.max(parts[s], axis=0, keepdims=True)
            top = jnp.maximum(top, jnp.where(base + s < count, here, -FAR))
        top = jnp.where(base < count, top, 0.0)
        probs = []
        total = jnp.zeros((1, wide), jnp.float32)
        for s in range(GROUP):
            level = top + jnp.where(base + s < count, 0.0, FAR)
            p = jnp.exp2((parts[s] - level) * SCALE2)
            total = total + jnp.sum(p, axis=0, keepdims=True)
            probs.append(p.astype(jnp.bfloat16))
        vals = jnp.concatenate([v[i] for i in ids], axis=0)
        summed = lax.dot_general(
            vals,
            jnp.concatenate(probs, axis=0),
            (((0,), (0,)), ((), ())),
            preferred_element_type=jnp.float32,
        )
        return top, total, summed

    def step(g, carry):
        counts = []
        for u in range(unroll):
            counts.append(pick(u, g * unroll + u))
        for u in range(unroll):
            tops[u], totals[u], sums[u] = chunk(u, g * unroll + u, 0, counts[u])
        for u in range(unroll):

            @pl.when(counts[u] > GROUP)
            def _():
                top1, total1, sum1 = chunk(u, g * unroll + u, GROUP, counts[u])
                top0 = tops[u]
                both = jnp.maximum(top0, top1)
                scale0 = jnp.exp2((top0 - both) * SCALE2)
                scale1 = jnp.exp2((top1 - both) * SCALE2)
                tops[u] = both
                totals[u] = totals[u] * scale0 + total1 * scale1
                sums[u] = sums[u] * scale0 + sum1 * scale1

        for u in range(unroll):
            r = g * unroll + u
            total = totals[u]
            seen = total > 0
            safe = jnp.where(seen, total, 1.0)
            level = jnp.where(seen, tops[u] * SCALE2 + jnp.log2(safe), -FAR)
            result = (sums[u] * (1.0 / safe)).astype(jnp.bfloat16)
            position = r * BLOCK + lax.broadcasted_iota(jnp.int32, (1, HD), 1)
            mine = position >= starts[r]
            lse[r, :, :HD] = jnp.where(mine, level[:, :HD], lse[r, :, :HD])
            old = out[r, :, :HD].astype(jnp.float32)
            new = result[:, :HD].astype(jnp.float32)
            out[r, :, :HD] = jnp.where(mine, new, old).astype(jnp.bfloat16)
            lse[r, :, HD:] = level[:, HD:BLOCK]
            out[r, :, HD:] = result[:, HD:BLOCK]

            @pl.when(r < requests - 1)
            def _():
                lse[r + 1, :, :HD] = level[:, BLOCK:]
                out[r + 1, :, :HD] = result[:, BLOCK:]

        return carry

    lax.fori_loop(0, requests // unroll, step, 0)


def partial_attention(q, k, v, block_imgs, img_req, req_start):
    tokens = q.shape[0]
    unroll = 2
    wide = BLOCK + HD
    smem = pl.BlockSpec(memory_space=pltpu.SMEM)
    vmem = pl.BlockSpec(memory_space=pltpu.VMEM)

    def kernel(*refs):
        partial_kernel(unroll, *refs)

    return pl.pallas_call(
        kernel,
        out_shape=(
            jax.ShapeDtypeStruct((tokens // BLOCK, HD, BLOCK), jnp.bfloat16),
            jax.ShapeDtypeStruct((tokens // BLOCK, 1, BLOCK), jnp.float32),
        ),
        in_specs=[smem, smem, smem, vmem, vmem, vmem],
        out_specs=(vmem, vmem),
        scratch_shapes=[
            pltpu.SMEM((unroll, 16), jnp.int32),
            pltpu.VMEM((unroll, 1, wide), jnp.float32),
            pltpu.VMEM((unroll, 1, wide), jnp.float32),
            pltpu.VMEM((unroll, HD, wide), jnp.float32),
        ],
        name="partial",
    )(block_imgs, img_req, req_start, q, k, v)


NX = 4
NZ = 8
MESH = pl.DeviceIdType.MESH


def push(src, dst, sent, landed, ctx, cache):
    return pltpu.make_async_remote_copy(
        src_ref=src,
        dst_ref=dst,
        send_sem=sent,
        recv_sem=landed,
        device_id=(ctx, cache),
        device_id_type=MESH,
    )


def turn(i):
    return 0 if i == 0 else ((i + 1) // 2 if i % 2 else NZ - i // 2)


def place():
    c = lax.axis_index("ctx")
    y = lax.axis_index("cache")
    return c, y, c // (2 * NZ), lax.rem(c // 2, NZ), lax.rem(c, 2)


def greet(c, y, offsets):
    barrier = pltpu.get_barrier_semaphore()

    def ring(s, carry):
        pl.semaphore_signal(
            barrier, inc=1, device_id=(lax.rem(c + s, 2 * NX * NZ), y), device_id_type=MESH
        )
        return carry

    lax.fori_loop(1, 2 * NX * NZ, ring, 0)
    for o in offsets:
        pl.semaphore_signal(
            barrier, inc=1, device_id=(c, lax.rem(y + o, 4)), device_id_type=MESH
        )
    pl.semaphore_wait(barrier, 2 * NX * NZ - 1 + len(offsets))


def share(buf, sems, c, y, z, part):
    sent, came, left, right, far = sems
    up = lax.rem(y + 1, 4)
    down = lax.rem(y + 3, 4)

    def piece(dz, who):
        return buf.at[:, lax.rem(z + NZ - dz, NZ), :, pl.ds(who * part, part), :]

    def forward(i):
        dz = turn(i)
        own = piece(dz, y)
        push(own, own, sent.at[0, dz], came.at[dz], c, up).wait_recv()
        push(own, own, sent.at[0, dz], left.at[dz], c, up).start()
        push(own, own, sent.at[1, dz], right.at[dz], c, down).start()

    def relay(i):
        dz = turn(i)
        if i % 2 == 0:
            got = piece(dz, down)
            push(got, got, sent.at[2, dz], left.at[dz], c, up).wait_recv()
            push(got, got, sent.at[2, dz], far.at[dz], c, up).start()
        else:
            got = piece(dz, up)
            push(got, got, sent.at[2, dz], right.at[dz], c, down).wait_recv()
            push(got, got, sent.at[2, dz], far.at[dz], c, down).start()

    def finish(i):
        dz = turn(i)
        if i % 2 == 0:
            got = piece(dz, up)
            push(got, got, sent.at[2, dz], right.at[dz], c, down).wait_recv()
        else:
            got = piece(dz, down)
            push(got, got, sent.at[2, dz], left.at[dz], c, up).wait_recv()
        got = piece(dz, lax.rem(y + 2, 4))
        push(got, got, sent.at[2, dz], far.at[dz], c, up).wait_recv()
        own = piece(dz, y)
        for k in range(3):
            push(own, own, sent.at[k, dz], far.at[dz], c, up).wait_send()

    return forward, relay, finish


def spread_kernel(part, q, buf, out_sem, sent, came, left, right, far):
    c, y, x, z, core = place()
    greet(c, y, (1, 3))
    rows = pl.ds(y * part, part)
    mine = buf.at[x, z, core, rows, :]

    def block(to):
        return q.at[rows, pl.ds(pl.multiple_of(to * HD, HD), HD)]

    for i in range(NZ):
        dz = turn(i)

        def send(j, carry):
            to = (
                lax.rem(x + j // 2, NX) * (2 * NZ)
                + lax.rem(z + dz, NZ) * 2
                + lax.rem(core + lax.rem(j, 2), 2)
            )
            push(block(to), mine, out_sem.at[dz], came.at[dz], to, y).start()
            return carry

        if i == 0:
            pltpu.make_async_copy(block(c), mine, came.at[0]).start()
        lax.fori_loop(1 if i == 0 else 0, 2 * NX, send, 0)
    forward, relay, finish = share(buf, (sent, came, left, right, far), c, y, z, part)
    for i in range(NZ + 1):
        if i < NZ:
            forward(i)
        if i >= 1:
            relay(i - 1)
    for i in range(NZ):
        dz = turn(i)
        finish(i)
        whole = buf.at[:, z, :, rows, :]
        if i == 0:
            some = q.at[rows, pl.ds(0, (2 * NX - 1) * HD)]
            push(some, some, out_sem.at[dz], came.at[dz], c, y).wait_send()
        else:
            push(whole, whole, out_sem.at[dz], came.at[dz], c, y).wait_send()


def spread(queries, part):
    def kernel(*refs):
        spread_kernel(part, *refs)

    dma = pltpu.SemaphoreType.DMA
    return pl.pallas_call(
        kernel,
        out_shape=jax.ShapeDtypeStruct((NX, NZ, 2, 4 * part, HD), jnp.bfloat16),
        in_specs=[pl.BlockSpec(memory_space=pl.ANY)],
        out_specs=pl.BlockSpec(memory_space=pltpu.VMEM),
        scratch_shapes=[dma((NZ,)), dma((3, NZ)), dma((NZ,)), dma((NZ,)), dma((NZ,)), dma((NZ,))],
        compiler_params=pltpu.CompilerParams(collective_id=1, has_side_effects=True),
        name="spread",
    )(queries)


def merge_kernel(
    deep, part, lse, buf, levels, alpha, relayed, raw, added, adding, final,
    lse_sent, lse_came, a_sent, a_came, r_sent, r_came, m_sent, m_came,
    out_sem, came, sent, left, right, far,
):
    c, y, x, z, core = place()
    up = lax.rem(y + 1, 4)
    down = lax.rem(y + 3, 4)
    across = lax.rem(y + 2, 4)
    greet(c, y, (1, 2, 3))

    def rows(who):
        return pl.ds(pl.multiple_of(who * deep, deep), deep)

    def chip(i):
        return lax.rem(z + turn(i), NZ)

    own_lse = pltpu.make_async_copy(lse, levels.at[y], lse_came.at[3])
    own_lse.start()
    tell = [
        push(lse, levels.at[y], lse_sent.at[o - 1], lse_came.at[o - 1], c, lax.rem(y + o, 4))
        for o in (1, 2, 3)
    ]
    for t in tell:
        t.start()

    def offers(i):
        zs = chip(i)
        return (
            push(part.at[pl.ds(0, 2), zs, rows(across), :], relayed.at[0, i],
                 a_sent.at[0, i], a_came.at[0, i], c, up),
            push(part.at[pl.ds(2, 2), zs, rows(across), :], relayed.at[1, i],
                 a_sent.at[1, i], a_came.at[1, i], c, down),
            push(part.at[pl.ds(2, 2), zs, rows(up), :], raw.at[0, i],
                 r_sent.at[0, i], r_came.at[0, i], c, up),
            push(part.at[pl.ds(0, 2), zs, rows(down), :], raw.at[1, i],
                 r_sent.at[1, i], r_came.at[1, i], c, down),
        )

    offered = [offers(i) for i in range(NZ)]

    def offer(i):
        for p in offered[i]:
            p.start()

    def adds(i):
        return (
            push(adding.at[0, i], added.at[0, i], m_sent.at[0, i], m_came.at[0, i], c, up),
            push(adding.at[1, i], added.at[1, i], m_sent.at[1, i], m_came.at[1, i], c, down),
        )

    added_to = [adds(i) for i in range(NZ)]

    def weigh(who, k, zs, block):
        return block.astype(jnp.float32) * alpha[who, k * NZ + zs]

    def add(i):
        zs = chip(i)
        ready = offered[i]
        ready[0].wait_recv()
        ready[1].wait_recv()
        for k in range(2):
            adding[0, i, k] = (
                weigh(down, k, zs, relayed[0, i, k]) + weigh(y, k, zs, part[k, zs, rows(up), :])
            ).astype(jnp.bfloat16)
            adding[1, i, k] = (
                weigh(up, k + 2, zs, relayed[1, i, k])
                + weigh(y, k + 2, zs, part[k + 2, zs, rows(down), :])
            ).astype(jnp.bfloat16)

    def complete(i):
        zs = chip(i)
        ready = offered[i]
        ready[2].wait_recv()
        ready[3].wait_recv()
        for p in added_to[i]:
            p.wait_recv()
        for k in range(2):
            final[i, k] = (
                weigh(y, k, zs, part[k, zs, rows(y), :])
                + added[0, i, k].astype(jnp.float32)
                + weigh(up, k, zs, raw[1, i, k])
            ).astype(jnp.bfloat16)
            final[i, k + 2] = (
                weigh(y, k + 2, zs, part[k + 2, zs, rows(y), :])
                + added[1, i, k].astype(jnp.float32)
                + weigh(down, k + 2, zs, raw[0, i, k])
            ).astype(jnp.bfloat16)

    mine = buf.at[x, z, core, pl.ds(y * deep, deep), :]

    def scatter(i):
        dz = turn(i)
        zs = chip(i)

        def block(to_x, to_core):
            return final.at[i, to_x, :, pl.ds(pl.multiple_of(to_core * HD, HD), HD)]

        def send(j, carry):
            to_x = lax.rem(x + j // 2, NX)
            to_core = lax.rem(core + lax.rem(j, 2), 2)
            to = to_x * (2 * NZ) + zs * 2 + to_core
            push(block(to_x, to_core), mine, out_sem.at[dz], came.at[dz], to, y).start()
            return carry

        if i == 0:
            pltpu.make_async_copy(block(x, core), mine, came.at[0]).start()
        lax.fori_loop(1 if i == 0 else 0, 2 * NX, send, 0)

    forward, relay, finish = share(buf, (sent, came, left, right, far), c, y, z, deep)
    for i in range(4):
        offer(i)
    own_lse.wait()
    for t in tell:
        t.wait_recv()
    tops = jnp.maximum(
        jnp.maximum(levels[0], levels[1]), jnp.maximum(levels[2], levels[3])
    )
    weights = [jnp.exp2(levels[k] - tops) for k in range(4)]
    scale = 1.0 / (weights[0] + weights[1] + weights[2] + weights[3])
    for k in range(4):
        alpha[k] = weights[k] * scale
    lead, done, onward, last = 4, 2, 4, 5
    for t in range(NZ + last):
        if t + lead < NZ:
            offer(t + lead)
        if t < NZ:
            add(t)
        if 0 <= t - done < NZ:
            complete(t - done)
        if t < NZ:
            for p in added_to[t]:
                p.start()
        if 0 <= t - done < NZ:
            scatter(t - done)
        if 0 <= t - onward < NZ:
            forward(t - onward)
        if 0 <= t - last < NZ:
            relay(t - last)
    for i in range(NZ):
        dz = turn(i)
        finish(i)
        for p in offered[i] + added_to[i]:
            p.wait_send()
        if i == 0:
            some = buf.at[0, pl.ds(0, 2 * NX - 1), 0, pl.ds(0, deep), :]
            push(some, some, out_sem.at[dz], came.at[dz], c, y).wait_send()
        else:
            push(final.at[i], final.at[i], out_sem.at[dz], came.at[dz], c, y).wait_send()
    for t in tell:
        t.wait_send()


def merge(parts, lse, deep):
    def kernel(*refs):
        merge_kernel(deep, *refs)

    dma = pltpu.SemaphoreType.DMA
    vmem = pl.BlockSpec(memory_space=pltpu.VMEM)
    half = (2, NZ, 2, deep, BLOCK)
    return pl.pallas_call(
        kernel,
        out_shape=jax.ShapeDtypeStruct((NX, NZ, 2, HD, HD), jnp.bfloat16),
        in_specs=[vmem, vmem],
        out_specs=vmem,
        scratch_shapes=[
            pltpu.VMEM((4, NX * NZ, 1, BLOCK), jnp.float32),
            pltpu.VMEM((4, NX * NZ, 1, BLOCK), jnp.float32),
            pltpu.VMEM(half, jnp.bfloat16),
            pltpu.VMEM(half, jnp.bfloat16),
            pltpu.VMEM(half, jnp.bfloat16),
            pltpu.VMEM(half, jnp.bfloat16),
            pltpu.VMEM((NZ, NX, deep, BLOCK), jnp.bfloat16),
            dma((3,)), dma((4,)),
            dma((2, NZ)), dma((2, NZ)), dma((2, NZ)), dma((2, NZ)), dma((2, NZ)), dma((2, NZ)),
            dma((NZ,)), dma((NZ,)), dma((3, NZ)), dma((NZ,)), dma((NZ,)), dma((NZ,)),
        ],
        compiler_params=pltpu.CompilerParams(collective_id=2, has_side_effects=True),
        name="merge",
    )(parts, lse)


def turn_kernel(src, dst):
    for k in range(src.shape[0]):
        dst[:, k * HD : (k + 1) * HD] = src[k].T


def turned(heads):
    count, _, rows = heads.shape
    step = 8
    return pl.pallas_call(
        turn_kernel,
        grid=(count // step,),
        out_shape=jax.ShapeDtypeStruct((rows, count * HD), heads.dtype),
        in_specs=[pl.BlockSpec((step, HD, rows), lambda i: (i, 0, 0))],
        out_specs=pl.BlockSpec((rows, step * HD), lambda i: (0, i)),
        name="turned",
    )(heads)


def shards(queries, keys, values, block_imgs, img_req, req_start):
    ctx = lax.axis_size("ctx")
    cache = lax.axis_size("cache")
    rows = queries.shape[0]
    part = rows // cache
    tokens = rows * ctx
    q = spread(queries, part).reshape(tokens, HD)
    out, lse = partial_attention(q, keys, values, block_imgs.T, img_req, req_start)
    deep = HD // cache
    heads = merge(out.reshape(NX, NZ, HD, BLOCK), lse, deep)
    return turned(heads.reshape(ctx, HD, rows))


def solution(mesh):
    placed = (P("ctx", None), P("cache", None, "ctx"), P("cache", None, "ctx"), P(), P(), P())
    return jax.shard_map(
        shards, mesh=mesh, in_specs=placed, out_specs=P("ctx", None), check_vma=False
    )
```

```python
import jax
import jax.numpy as jnp
from jax import lax
from jax.experimental import pallas as pl
from jax.experimental.pallas import tpu as pltpu
from jax.sharding import PartitionSpec as P

HD = 128
BLOCK = 256
NX = 4
NZ = 8
FAR = 1e30
SCALE2 = HD ** (-0.5) * 1.4426950408889634
MESH = pl.DeviceIdType.MESH
RELAY, WORK, ADD, DONE, ONWARD, LAST = 1, 3, 5, 7, 9, 10


def push(src, dst, sent, landed, ctx, cache):
    return pltpu.make_async_remote_copy(
        src_ref=src,
        dst_ref=dst,
        send_sem=sent,
        recv_sem=landed,
        device_id=(ctx, cache),
        device_id_type=MESH,
    )


def turn(i):
    return 0 if i == 0 else ((i + 1) // 2 if i % 2 else NZ - i // 2)


def greet(c, y, offsets):
    barrier = pltpu.get_barrier_semaphore()

    def ring(s, carry):
        pl.semaphore_signal(
            barrier, inc=1, device_id=(lax.rem(c + s, 2 * NX * NZ), y), device_id_type=MESH
        )
        return carry

    lax.fori_loop(1, 2 * NX * NZ, ring, 0)
    for o in offsets:
        pl.semaphore_signal(
            barrier, inc=1, device_id=(c, lax.rem(y + o, 4)), device_id_type=MESH
        )
    pl.semaphore_wait(barrier, 2 * NX * NZ - 1 + len(offsets))


def share(buf, sems, c, y, column, part):
    sent, came, left, right, far = sems
    up = lax.rem(y + 1, 4)
    down = lax.rem(y + 3, 4)

    def piece(i, who):
        return buf.at[:, column(i), :, pl.ds(who * part, part), :]

    def forward(i):
        own = piece(i, y)
        going = push(own, own, sent.at[0, i], left.at[i], c, up)
        push(own, own, sent.at[0, i], came.at[i], c, up).wait_recv()
        going.start()
        push(own, own, sent.at[1, i], right.at[i], c, down).start()

    def relay(i):
        if i % 2 == 0:
            got = piece(i, down)
            push(got, got, sent.at[2, i], left.at[i], c, up).wait_recv()
            push(got, got, sent.at[2, i], far.at[i], c, up).start()
        else:
            got = piece(i, up)
            push(got, got, sent.at[2, i], right.at[i], c, down).wait_recv()
            push(got, got, sent.at[2, i], far.at[i], c, down).start()

    def ready(i):
        if i % 2 == 0:
            got = piece(i, up)
            push(got, got, sent.at[2, i], right.at[i], c, down).wait_recv()
        else:
            got = piece(i, down)
            push(got, got, sent.at[2, i], left.at[i], c, up).wait_recv()
        got = piece(i, lax.rem(y + 2, 4))
        push(got, got, sent.at[2, i], far.at[i], c, up).wait_recv()

    def drain(i):
        own = piece(i, y)
        for k in range(3):
            push(own, own, sent.at[k, i], far.at[i], c, up).wait_send()

    return forward, relay, ready, drain


def score(rows, keys):
    return lax.dot_general(
        keys, rows, (((1,), (1,)), ((), ())), preferred_element_type=jnp.float32
    )


def weigh_values(vals, probs):
    return lax.dot_general(
        vals, probs, (((0,), (0,)), ((), ())), preferred_element_type=jnp.float32
    )


def attend_block(r, first, q0, q1, lists, owners, starts, k, v):
    held, lat, _ = k.shape
    images = owners.shape[0]
    slots = lists.shape[0] // 2
    sides = []
    for side in range(2):
        ids, gaps = [], []
        for s in range(slots):
            image = lists[side * slots + s, r]
            local = image - first
            owner = owners[jnp.minimum(image, images - 1)]
            here = (
                (image < images) & (owner == r - 1 + side) & (local >= 0) & (local < held)
            )
            ids.append(jnp.where(here, local, 0))
            gaps.append(jnp.where(here, 0.0, FAR))
        sides.append((ids, gaps))
    (old_ids, old_gaps), (ids, gaps) = sides
    keys = jnp.concatenate([k[i] for i in ids], axis=0)
    old_keys = jnp.concatenate([k[i] for i in old_ids], axis=0)
    new_scores = score(jnp.concatenate([q0, q1], axis=0), keys)
    old_scores = score(q0, old_keys)
    position = r * BLOCK + lax.broadcasted_iota(jnp.int32, (1, HD), 1)
    before = position < starts[r]
    probs = []
    halves = []
    for half in range(2):
        tile = []
        levels = []
        top = jnp.full((1, HD), -FAR, jnp.float32)
        for s in range(slots):
            span = slice(s * lat, (s + 1) * lat)
            if half == 0:
                block = jnp.where(before, old_scores[span], new_scores[span, :HD])
                gap = jnp.where(before, old_gaps[s], gaps[s])
            else:
                block = new_scores[span, HD:]
                gap = jnp.full((1, HD), gaps[s], jnp.float32)
            tile.append(block)
            levels.append(gap)
            top = jnp.maximum(top, jnp.max(block, axis=0, keepdims=True) - gap)
        top = jnp.where(top < -0.5 * FAR, 0.0, top)
        total = jnp.zeros((1, HD), jnp.float32)
        weights = []
        for s in range(slots):
            p = jnp.exp2((tile[s] - (top + levels[s])) * SCALE2)
            total = total + jnp.sum(p, axis=0, keepdims=True)
            weights.append(p.astype(jnp.bfloat16))
        probs.append(jnp.concatenate(weights, axis=0))
        halves.append((top, total))
    vals = jnp.concatenate([v[i] for i in ids], axis=0)
    old_vals = jnp.concatenate([v[i] for i in old_ids], axis=0)
    summed = weigh_values(vals, jnp.concatenate(probs, axis=1))
    old_summed = weigh_values(old_vals, probs[0])
    results = []
    for half in range(2):
        top, total = halves[half]
        seen = total > 0
        safe = jnp.where(seen, total, 1.0)
        level = jnp.where(seen, top * SCALE2 + jnp.log2(safe), -FAR)
        numer = summed[:, half * HD : (half + 1) * HD]
        if half == 0:
            numer = jnp.where(before, old_summed, numer)
        results.append((level, (numer * (1.0 / safe)).astype(jnp.bfloat16)))
    return results


def whole_kernel(
    part, lists, owners, starts, q, k_hbm, v_hbm, buf,
    qbuf, k, v, own, levels, alpha, relayed, raw, added, adding, final,
    kv_sem, q_out, q_came, q_sent, q_left, q_right, q_far,
    l_sent, l_came, a_sent, a_came, r_sent, r_came, m_sent, m_came,
    o_out, o_came, o_sent, o_left, o_right, o_far,
):
    c = lax.axis_index("ctx")
    y = lax.axis_index("cache")
    x = c // (2 * NZ)
    z = lax.rem(c // 2, NZ)
    core = lax.rem(c, 2)
    up = lax.rem(y + 1, 4)
    down = lax.rem(y + 3, 4)
    across = lax.rem(y + 2, 4)
    first = y * k.shape[0]
    rows = pl.ds(y * part, part)
    loads = [
        pltpu.make_async_copy(k_hbm, k, kv_sem.at[0]),
        pltpu.make_async_copy(v_hbm, v, kv_sem.at[1]),
    ]
    for load in loads:
        load.start()
    greet(c, y, (1, 2, 3))

    def behind(i):
        return lax.rem(z + NZ - turn(i), NZ)

    def ahead(i):
        return lax.rem(z + turn(i), NZ)

    def everyone(one, i):
        def send(j, carry):
            to_x = lax.rem(x + j // 2, NX)
            to_core = lax.rem(core + lax.rem(j, 2), 2)
            one(to_x, to_core)
            return carry

        lax.fori_loop(1 if i == 0 else 0, 2 * NX, send, 0)

    q_home = qbuf.at[x, z, core, rows, :]

    def q_block(to):
        return q.at[rows, pl.ds(pl.multiple_of(to * HD, HD), HD)]

    for i in range(NZ):

        def q_send(to_x, to_core):
            to = to_x * (2 * NZ) + ahead(i) * 2 + to_core
            push(q_block(to), q_home, q_out.at[i], q_came.at[i], to, y).start()

        if i == 0:
            pltpu.make_async_copy(q_block(c), q_home, q_came.at[0]).start()
        everyone(q_send, i)
    q_forward, q_relay, q_ready, q_drain = share(
        qbuf, (q_sent, q_came, q_left, q_right, q_far), c, y, behind, part
    )

    def work(i):
        q_ready(i)
        if i == 0:
            for load in loads:
                load.wait()
        zs = behind(i)

        def one(n, carry):
            results = attend_block(
                n * NZ + zs, first, qbuf[n, zs, 0], qbuf[n, zs, 1], lists, owners, starts, k, v
            )
            for half in range(2):
                level, block = results[half]
                levels[y, i, n, :, half * HD : (half + 1) * HD] = level
                own[i, n, :, half * HD : (half + 1) * HD] = block
            return carry

        lax.fori_loop(0, NX, one, 0)

    def deep(who):
        return pl.ds(pl.multiple_of(who * part, part), part)

    low, high = pl.ds(0, 2), pl.ds(2, 2)
    tell = [
        [
            push(levels.at[y, i], levels.at[y, i], l_sent.at[o - 1, i], l_came.at[o - 1, i],
                 c, lax.rem(y + o, 4))
            for o in (1, 2, 3)
        ]
        for i in range(NZ)
    ]
    offers = [
        (
            push(own.at[i, low, deep(across), :], relayed.at[0, i],
                 a_sent.at[0, i], a_came.at[0, i], c, up),
            push(own.at[i, high, deep(across), :], relayed.at[1, i],
                 a_sent.at[1, i], a_came.at[1, i], c, down),
            push(own.at[i, high, deep(up), :], raw.at[0, i],
                 r_sent.at[0, i], r_came.at[0, i], c, up),
            push(own.at[i, low, deep(down), :], raw.at[1, i],
                 r_sent.at[1, i], r_came.at[1, i], c, down),
        )
        for i in range(NZ)
    ]
    adds = [
        (
            push(adding.at[0, i], added.at[0, i], m_sent.at[0, i], m_came.at[0, i], c, up),
            push(adding.at[1, i], added.at[1, i], m_sent.at[1, i], m_came.at[1, i], c, down),
        )
        for i in range(NZ)
    ]

    def offer(i):
        for p in tell[i] + list(offers[i]):
            p.start()

    def weigh(who, i, n, block):
        return block.astype(jnp.float32) * alpha[who, i, n]

    def add(i):
        for p in tell[i]:
            p.wait_recv()
        tops = jnp.maximum(
            jnp.maximum(levels[0, i], levels[1, i]), jnp.maximum(levels[2, i], levels[3, i])
        )
        weights = [jnp.exp2(levels[w, i] - tops) for w in range(4)]
        scale = 1.0 / (weights[0] + weights[1] + weights[2] + weights[3])
        for w in range(4):
            alpha[w, i] = weights[w] * scale
        offers[i][0].wait_recv()
        offers[i][1].wait_recv()
        for n in range(2):
            adding[0, i, n] = (
                weigh(down, i, n, relayed[0, i, n]) + weigh(y, i, n, own[i, n, deep(up), :])
            ).astype(jnp.bfloat16)
            adding[1, i, n] = (
                weigh(up, i, n + 2, relayed[1, i, n])
                + weigh(y, i, n + 2, own[i, n + 2, deep(down), :])
            ).astype(jnp.bfloat16)

    def complete(i):
        offers[i][2].wait_recv()
        offers[i][3].wait_recv()
        for p in adds[i]:
            p.wait_recv()
        for n in range(2):
            final[i, n] = (
                weigh(y, i, n, own[i, n, deep(y), :])
                + added[0, i, n].astype(jnp.float32)
                + weigh(up, i, n, raw[1, i, n])
            ).astype(jnp.bfloat16)
            final[i, n + 2] = (
                weigh(y, i, n + 2, own[i, n + 2, deep(y), :])
                + added[1, i, n].astype(jnp.float32)
                + weigh(down, i, n + 2, raw[0, i, n])
            ).astype(jnp.bfloat16)

    o_home = buf.at[x, z, core, rows, :]

    def o_block(i, to_x, to_core):
        return final.at[i, to_x, :, pl.ds(pl.multiple_of(to_core * HD, HD), HD)]

    def scatter(i):
        def o_send(to_x, to_core):
            to = to_x * (2 * NZ) + behind(i) * 2 + to_core
            push(o_block(i, to_x, to_core), o_home, o_out.at[i], o_came.at[i], to, y).start()

        if i == 0:
            pltpu.make_async_copy(o_block(0, x, core), o_home, o_came.at[0]).start()
        everyone(o_send, i)

    o_forward, o_relay, o_ready, o_drain = share(
        buf, (o_sent, o_came, o_left, o_right, o_far), c, y, ahead, part
    )

    def at(t, lag):
        return 0 <= t - lag < NZ

    for t in range(NZ + LAST):
        if at(t, 0):
            q_forward(t)
        if at(t, RELAY):
            q_relay(t - RELAY)
        if at(t, WORK):
            work(t - WORK)
        if at(t, ADD):
            add(t - ADD)
        if at(t, DONE):
            complete(t - DONE)
        if at(t, WORK):
            offer(t - WORK)
        if at(t, ADD):
            for p in adds[t - ADD]:
                p.start()
        if at(t, DONE):
            scatter(t - DONE)
        if at(t, ONWARD):
            o_forward(t - ONWARD)
        if at(t, LAST):
            o_relay(t - LAST)
    for i in range(NZ):
        o_ready(i)
        for p in tell[i] + list(offers[i]) + list(adds[i]):
            p.wait_send()
        for which, out, came in ((q_drain, q_out, q_came), (o_drain, o_out, o_came)):
            which(i)
            if i == 0:
                some = buf.at[0, pl.ds(0, 2 * NX - 1), 0, pl.ds(0, part), :]
            else:
                some = buf.at[0, :, 0, pl.ds(0, part), :]
            push(some, some, out.at[i], came.at[i], c, y).wait_send()


def whole(queries, keys, values, lists, img_req, req_start, part):
    def kernel(*refs):
        whole_kernel(part, *refs)

    dma = pltpu.SemaphoreType.DMA
    smem = pl.BlockSpec(memory_space=pltpu.SMEM)
    far = pl.BlockSpec(memory_space=pl.ANY)
    half = pltpu.VMEM((2, NZ, 2, part, BLOCK), jnp.bfloat16)
    heads = (NX, NZ, 2, HD, HD)
    level = pltpu.VMEM((4, NZ, NX, 1, BLOCK), jnp.float32)
    one, two, three = dma((NZ,)), dma((2, NZ)), dma((3, NZ))
    return pl.pallas_call(
        kernel,
        out_shape=jax.ShapeDtypeStruct(heads, jnp.bfloat16),
        in_specs=[smem, smem, smem, far, far, far],
        out_specs=pl.BlockSpec(memory_space=pltpu.VMEM),
        scratch_shapes=[
            pltpu.VMEM(heads, jnp.bfloat16),
            pltpu.VMEM(keys.shape, jnp.bfloat16),
            pltpu.VMEM(keys.shape, jnp.bfloat16),
            pltpu.VMEM((NZ, NX, HD, BLOCK), jnp.bfloat16),
            level, level, half, half, half, half,
            pltpu.VMEM((NZ, NX, part, BLOCK), jnp.bfloat16),
            dma((2,)), one, one, three, one, one, one,
            three, three, two, two, two, two, two, two,
            one, one, three, one, one, one,
        ],
        compiler_params=pltpu.CompilerParams(collective_id=1, has_side_effects=True),
        name="whole",
    )(lists, img_req, req_start, queries, keys, values)


def turn_kernel(src, dst):
    row = lax.broadcasted_iota(jnp.int32, (HD, HD), 0)
    column = lax.broadcasted_iota(jnp.int32, (HD, HD), 1)
    unit = (row == column).astype(jnp.bfloat16)
    count = src.shape[0]
    flat = src[...].reshape(count * HD, HD)
    dst[...] = lax.dot_general(
        unit, flat, (((1,), (1,)), ((), ())), preferred_element_type=jnp.float32
    ).astype(jnp.bfloat16)


def turned(heads):
    count, _, rows = heads.shape
    step = 16
    return pl.pallas_call(
        turn_kernel,
        grid=(count // step,),
        out_shape=jax.ShapeDtypeStruct((rows, count * HD), heads.dtype),
        in_specs=[pl.BlockSpec((step, HD, rows), lambda i: (i, 0, 0))],
        out_specs=pl.BlockSpec((rows, step * HD), lambda i: (0, i)),
        name="turned",
    )(heads)


def shards(queries, keys, values, block_imgs, img_req, req_start):
    ctx = lax.axis_size("ctx")
    rows = queries.shape[0]
    part = rows // lax.axis_size("cache")
    heads = whole(queries, keys, values, block_imgs.T, img_req, req_start, part)
    return turned(heads.reshape(ctx, HD, rows))


def solution(mesh):
    placed = (P("ctx", None), P("cache", None, "ctx"), P("cache", None, "ctx"), P(), P(), P())
    return jax.shard_map(
        shards, mesh=mesh, in_specs=placed, out_specs=P("ctx", None), check_vma=False
    )
```

```python
import jax
import jax.numpy as jnp
from jax import lax
from jax.experimental import pallas as pl
from jax.experimental.pallas import tpu as pltpu
from jax.sharding import PartitionSpec as P

HD = 128
BLOCK = 256
NX = 4
NZ = 8
FAR = 1e30
SCALE2 = HD ** (-0.5) * 1.4426950408889634
MESH = pl.DeviceIdType.MESH
RELAY, WORK, ADD, DONE, ONWARD, LAST, TURN = 3, 6, 9, 12, 15, 17, 19
DIRECT = ()


def push(src, dst, sent, landed, ctx, cache):
    return pltpu.make_async_remote_copy(
        src_ref=src,
        dst_ref=dst,
        send_sem=sent,
        recv_sem=landed,
        device_id=(ctx, cache),
        device_id_type=MESH,
    )


def turn(i):
    return 0 if i == 0 else ((i + 1) // 2 if i % 2 else NZ - i // 2)


def greet(c, y, offsets):
    barrier = pltpu.get_barrier_semaphore()

    def ring(s, carry):
        pl.semaphore_signal(
            barrier, inc=1, device_id=(lax.rem(c + s, 2 * NX * NZ), y), device_id_type=MESH
        )
        return carry

    lax.fori_loop(1, 2 * NX * NZ, ring, 0)
    for o in offsets:
        pl.semaphore_signal(
            barrier, inc=1, device_id=(c, lax.rem(y + o, 4)), device_id_type=MESH
        )
    pl.semaphore_wait(barrier, 2 * NX * NZ - 1 + len(offsets))


def share(buf, sems, c, y, column, part, direct=()):
    sent, came, left, right, far = sems
    up = lax.rem(y + 1, 4)
    down = lax.rem(y + 3, 4)

    def piece(i, who):
        return buf.at[:, column(i), :, pl.ds(who * part, part), :]

    def forward(i):
        own = piece(i, y)
        going = push(own, own, sent.at[0, i], left.at[i], c, up)
        push(own, own, sent.at[0, i], came.at[i], c, up).wait_recv()
        going.start()
        push(own, own, sent.at[1, i], right.at[i], c, down).start()

    def relay(i):
        if i in direct:
            return
        if i % 2 == 0:
            got = piece(i, down)
            push(got, got, sent.at[2, i], left.at[i], c, up).wait_recv()
            push(got, got, sent.at[2, i], far.at[i], c, up).start()
        else:
            got = piece(i, up)
            push(got, got, sent.at[2, i], right.at[i], c, down).wait_recv()
            push(got, got, sent.at[2, i], far.at[i], c, down).start()

    def ready(i):
        if i % 2 == 0 or i in direct:
            got = piece(i, up)
            push(got, got, sent.at[2, i], right.at[i], c, down).wait_recv()
        if i % 2 or i in direct:
            got = piece(i, down)
            push(got, got, sent.at[2, i], left.at[i], c, up).wait_recv()
        got = piece(i, lax.rem(y + 2, 4))
        push(got, got, sent.at[2, i], far.at[i], c, up).wait_recv()

    def drain(i):
        own = piece(i, y)
        for k in range(2 if i in direct else 3):
            push(own, own, sent.at[k, i], far.at[i], c, up).wait_send()

    return forward, relay, ready, drain


def score(rows, keys):
    return lax.dot_general(
        keys, rows, (((1,), (1,)), ((), ())), preferred_element_type=jnp.float32
    )


def weigh_values(vals, probs):
    return lax.dot_general(
        vals, probs, (((0,), (0,)), ((), ())), preferred_element_type=jnp.float32
    )


def attend_block(r, first, q0, q1, lists, owners, starts, k, v):
    held, lat, _ = k.shape
    images = owners.shape[0]
    slots = lists.shape[0] // 2
    sides = []
    for side in range(2):
        ids, gaps = [], []
        for s in range(slots):
            image = lists[side * slots + s, r]
            local = image - first
            owner = owners[jnp.minimum(image, images - 1)]
            here = (
                (image < images) & (owner == r - 1 + side) & (local >= 0) & (local < held)
            )
            ids.append(jnp.where(here, local, 0))
            gaps.append(jnp.where(here, 0.0, FAR))
        sides.append((ids, gaps))
    (old_ids, old_gaps), (ids, gaps) = sides
    keys = jnp.concatenate([k[i] for i in ids], axis=0)
    old_keys = jnp.concatenate([k[i] for i in old_ids], axis=0)
    new_scores = score(jnp.concatenate([q0, q1], axis=0), keys)
    old_scores = score(q0, old_keys)
    position = r * BLOCK + lax.broadcasted_iota(jnp.int32, (1, HD), 1)
    before = position < starts[r]
    probs = []
    halves = []
    for half in range(2):
        tile = []
        levels = []
        top = jnp.full((1, HD), -FAR, jnp.float32)
        for s in range(slots):
            span = slice(s * lat, (s + 1) * lat)
            if half == 0:
                block = jnp.where(before, old_scores[span], new_scores[span, :HD])
                gap = jnp.where(before, old_gaps[s], gaps[s])
            else:
                block = new_scores[span, HD:]
                gap = jnp.full((1, HD), gaps[s], jnp.float32)
            tile.append(block)
            levels.append(gap)
            top = jnp.maximum(top, jnp.max(block, axis=0, keepdims=True) - gap)
        top = jnp.where(top < -0.5 * FAR, 0.0, top)
        total = jnp.zeros((1, HD), jnp.float32)
        weights = []
        for s in range(slots):
            p = jnp.exp2((tile[s] - (top + levels[s])) * SCALE2)
            total = total + jnp.sum(p, axis=0, keepdims=True)
            weights.append(p.astype(jnp.bfloat16))
        probs.append(jnp.concatenate(weights, axis=0))
        halves.append((top, total))
    vals = jnp.concatenate([v[i] for i in ids], axis=0)
    old_vals = jnp.concatenate([v[i] for i in old_ids], axis=0)
    summed = weigh_values(vals, jnp.concatenate(probs, axis=1))
    old_summed = weigh_values(old_vals, probs[0])
    results = []
    for half in range(2):
        top, total = halves[half]
        seen = total > 0
        safe = jnp.where(seen, total, 1.0)
        level = jnp.where(seen, top * SCALE2 + jnp.log2(safe), -FAR)
        numer = summed[:, half * HD : (half + 1) * HD]
        if half == 0:
            numer = jnp.where(before, old_summed, numer)
        results.append((level, (numer * (1.0 / safe)).astype(jnp.bfloat16)))
    return results


def whole_kernel(
    part, lists, owners, starts, q, k_hbm, v_hbm, result,
    buf, qbuf, k, v, own, levels, alpha, relayed, raw, added, adding, final,
    kv_sem, q_out, q_more, q_came, q_sent, q_left, q_right, q_far,
    l_sent, l_came, a_sent, a_came, r_sent, r_came, m_sent, m_came,
    o_out, o_came, o_sent, o_left, o_right, o_far,
):
    c = lax.axis_index("ctx")
    y = lax.axis_index("cache")
    x = c // (2 * NZ)
    z = lax.rem(c // 2, NZ)
    core = lax.rem(c, 2)
    up = lax.rem(y + 1, 4)
    down = lax.rem(y + 3, 4)
    across = lax.rem(y + 2, 4)
    first = y * k.shape[0]
    rows = pl.ds(y * part, part)
    loads = [
        pltpu.make_async_copy(k_hbm, k, kv_sem.at[0]),
        pltpu.make_async_copy(v_hbm, v, kv_sem.at[1]),
    ]
    for load in loads:
        load.start()
    greet(c, y, (1, 2, 3))

    def behind(i):
        return lax.rem(z + NZ - turn(i), NZ)

    def ahead(i):
        return lax.rem(z + turn(i), NZ)

    def everyone(one, i):
        def send(j, carry):
            to_x = lax.rem(x + j // 2, NX)
            to_core = lax.rem(core + lax.rem(j, 2), 2)
            one(to_x, to_core)
            return carry

        lax.fori_loop(1 if i == 0 else 0, 2 * NX, send, 0)

    def q_hand(i, who, out, came):
        span = pl.ds(pl.multiple_of(who * part, part), part)
        home = qbuf.at[x, z, core, span, :]

        def block(to):
            return q.at[span, pl.ds(pl.multiple_of(to * HD, HD), HD)]

        def q_send(to_x, to_core):
            to = to_x * (2 * NZ) + ahead(i) * 2 + to_core
            push(block(to), home, out.at[i], came.at[i], to, y).start()

        if i == 0:
            pltpu.make_async_copy(block(c), home, came.at[0]).start()
        everyone(q_send, i)

    for i in range(NZ):
        q_hand(i, y, q_out, q_came)
    for i in DIRECT:
        q_hand(i, across, q_more, q_far)
    q_forward, q_relay, q_ready, q_drain = share(
        qbuf, (q_sent, q_came, q_left, q_right, q_far), c, y, behind, part, DIRECT
    )

    def work(i):
        q_ready(i)
        if i == 0:
            for load in loads:
                load.wait()
        zs = behind(i)

        def one(n, carry):
            results = attend_block(
                n * NZ + zs, first, qbuf[n, zs, 0], qbuf[n, zs, 1], lists, owners, starts, k, v
            )
            for half in range(2):
                level, block = results[half]
                levels[y, i, n, :, half * HD : (half + 1) * HD] = level
                own[i, n, :, half * HD : (half + 1) * HD] = block
            return carry

        lax.fori_loop(0, NX, one, 0)

    def deep(who):
        return pl.ds(pl.multiple_of(who * part, part), part)

    low, high = pl.ds(0, 2), pl.ds(2, 2)
    tell = [
        [
            push(levels.at[y, i], levels.at[y, i], l_sent.at[o - 1, i], l_came.at[o - 1, i],
                 c, lax.rem(y + o, 4))
            for o in (1, 2, 3)
        ]
        for i in range(NZ)
    ]
    offers = [
        (
            push(own.at[i, low, deep(across), :], relayed.at[0, i],
                 a_sent.at[0, i], a_came.at[0, i], c, up),
            push(own.at[i, high, deep(across), :], relayed.at[1, i],
                 a_sent.at[1, i], a_came.at[1, i], c, down),
            push(own.at[i, high, deep(up), :], raw.at[0, i],
                 r_sent.at[0, i], r_came.at[0, i], c, up),
            push(own.at[i, low, deep(down), :], raw.at[1, i],
                 r_sent.at[1, i], r_came.at[1, i], c, down),
        )
        for i in range(NZ)
    ]
    adds = [
        (
            push(adding.at[0, i], added.at[0, i], m_sent.at[0, i], m_came.at[0, i], c, up),
            push(adding.at[1, i], added.at[1, i], m_sent.at[1, i], m_came.at[1, i], c, down),
        )
        for i in range(NZ)
    ]

    def offer(i):
        for p in tell[i] + list(offers[i]):
            p.start()

    def weigh(who, i, n, block):
        return block.astype(jnp.float32) * alpha[who, i, n]

    def add(i):
        for p in tell[i]:
            p.wait_recv()
        tops = jnp.maximum(
            jnp.maximum(levels[0, i], levels[1, i]), jnp.maximum(levels[2, i], levels[3, i])
        )
        weights = [jnp.exp2(levels[w, i] - tops) for w in range(4)]
        scale = 1.0 / (weights[0] + weights[1] + weights[2] + weights[3])
        for w in range(4):
            alpha[w, i] = weights[w] * scale
        offers[i][0].wait_recv()
        offers[i][1].wait_recv()
        for n in range(2):
            adding[0, i, n] = (
                weigh(down, i, n, relayed[0, i, n]) + weigh(y, i, n, own[i, n, deep(up), :])
            ).astype(jnp.bfloat16)
            adding[1, i, n] = (
                weigh(up, i, n + 2, relayed[1, i, n])
                + weigh(y, i, n + 2, own[i, n + 2, deep(down), :])
            ).astype(jnp.bfloat16)

    def complete(i):
        offers[i][2].wait_recv()
        offers[i][3].wait_recv()
        for p in adds[i]:
            p.wait_recv()
        for n in range(2):
            final[i, n] = (
                weigh(y, i, n, own[i, n, deep(y), :])
                + added[0, i, n].astype(jnp.float32)
                + weigh(up, i, n, raw[1, i, n])
            ).astype(jnp.bfloat16)
            final[i, n + 2] = (
                weigh(y, i, n + 2, own[i, n + 2, deep(y), :])
                + added[1, i, n].astype(jnp.float32)
                + weigh(down, i, n + 2, raw[0, i, n])
            ).astype(jnp.bfloat16)

    o_home = buf.at[x, z, core, rows, :]

    def o_block(i, to_x, to_core):
        return final.at[i, to_x, :, pl.ds(pl.multiple_of(to_core * HD, HD), HD)]

    def scatter(i):
        def o_send(to_x, to_core):
            to = to_x * (2 * NZ) + behind(i) * 2 + to_core
            push(o_block(i, to_x, to_core), o_home, o_out.at[i], o_came.at[i], to, y).start()

        if i == 0:
            pltpu.make_async_copy(o_block(0, x, core), o_home, o_came.at[0]).start()
        everyone(o_send, i)

    o_forward, o_relay, o_ready, o_drain = share(
        buf, (o_sent, o_came, o_left, o_right, o_far), c, y, ahead, part
    )

    row = lax.broadcasted_iota(jnp.int32, (HD, HD), 0)
    column = lax.broadcasted_iota(jnp.int32, (HD, HD), 1)
    unit = (row == column).astype(jnp.bfloat16)

    def turned(i):
        o_ready(i)
        zs = ahead(i)
        for n in range(NX):
            heads = buf[n, zs].reshape(2 * HD, HD)
            to = pl.multiple_of((n * NZ + zs) * 2 * HD, 2 * HD)
            result[:, pl.ds(to, 2 * HD)] = score(heads, unit).astype(jnp.bfloat16)

    def at(t, lag):
        return 0 <= t - lag < NZ

    for t in range(NZ + TURN):
        if at(t, 0):
            q_forward(t)
        if at(t, RELAY):
            q_relay(t - RELAY)
        if at(t, WORK):
            work(t - WORK)
        if at(t, ADD):
            add(t - ADD)
        if at(t, DONE):
            complete(t - DONE)
        if at(t, WORK):
            offer(t - WORK)
        if at(t, ADD):
            for p in adds[t - ADD]:
                p.start()
        if at(t, DONE):
            scatter(t - DONE)
        if at(t, ONWARD):
            o_forward(t - ONWARD)
        if at(t, LAST):
            o_relay(t - LAST)
        if at(t, TURN):
            turned(t - TURN)
    for i in range(NZ):
        for p in tell[i] + list(offers[i]) + list(adds[i]):
            p.wait_send()
        for which, out, came in ((q_drain, q_out, q_came), (o_drain, o_out, o_came)):
            which(i)
            if i == 0:
                some = buf.at[0, pl.ds(0, 2 * NX - 1), 0, pl.ds(0, part), :]
            else:
                some = buf.at[0, :, 0, pl.ds(0, part), :]
            push(some, some, out.at[i], came.at[i], c, y).wait_send()
            if i in DIRECT and which is q_drain:
                push(some, some, q_more.at[i], came.at[i], c, y).wait_send()


def whole(queries, keys, values, lists, img_req, req_start, part):
    def kernel(*refs):
        whole_kernel(part, *refs)

    dma = pltpu.SemaphoreType.DMA
    smem = pl.BlockSpec(memory_space=pltpu.SMEM)
    far = pl.BlockSpec(memory_space=pl.ANY)
    half = pltpu.VMEM((2, NZ, 2, part, BLOCK), jnp.bfloat16)
    heads = (NX, NZ, 2, HD, HD)
    level = pltpu.VMEM((4, NZ, NX, 1, BLOCK), jnp.float32)
    one, two, three = dma((NZ,)), dma((2, NZ)), dma((3, NZ))
    return pl.pallas_call(
        kernel,
        out_shape=pltpu.VMEM((queries.shape[0], queries.shape[1]), jnp.bfloat16),
        in_specs=[smem, smem, smem, far, far, far],
        out_specs=pl.BlockSpec(memory_space=pltpu.VMEM),
        scratch_shapes=[
            pltpu.VMEM(heads, jnp.bfloat16),
            pltpu.VMEM(heads, jnp.bfloat16),
            pltpu.VMEM(keys.shape, jnp.bfloat16),
            pltpu.VMEM(keys.shape, jnp.bfloat16),
            pltpu.VMEM((NZ, NX, HD, BLOCK), jnp.bfloat16),
            level, level, half, half, half, half,
            pltpu.VMEM((NZ, NX, part, BLOCK), jnp.bfloat16),
            dma((2,)), one, one, one, three, one, one, one,
            three, three, two, two, two, two, two, two,
            one, one, three, one, one, one,
        ],
        compiler_params=pltpu.CompilerParams(collective_id=1, has_side_effects=True),
        name="whole",
    )(lists, img_req, req_start, queries, keys, values)


def shards(queries, keys, values, block_imgs, img_req, req_start):
    part = queries.shape[0] // lax.axis_size("cache")
    return whole(queries, keys, values, block_imgs.T, img_req, req_start, part)


def solution(mesh):
    placed = (P("ctx", None), P("cache", None, "ctx"), P("cache", None, "ctx"), P(), P(), P())
    return jax.shard_map(
        shards, mesh=mesh, in_specs=placed, out_specs=P("ctx", None), check_vma=False
    )
```

```python
import jax
import jax.numpy as jnp
from jax import lax
from jax.experimental import pallas as pl
from jax.experimental.pallas import tpu as pltpu
from jax.sharding import PartitionSpec as P

HD = 128
BLOCK = 256
NX = 4
NZ = 8
FAR = 1e30
SCALE2 = HD ** (-0.5) * 1.4426950408889634
MESH = pl.DeviceIdType.MESH
RELAY, WORK, ADD, DONE, ONWARD, LAST, TURN = 1, 2, 5, 8, 11, 13, 15
DIRECT = (0, 1, 2, 3, 4, 5, 6, 7)
PAIR = 4


def push(src, dst, sent, landed, ctx, cache):
    return pltpu.make_async_remote_copy(
        src_ref=src,
        dst_ref=dst,
        send_sem=sent,
        recv_sem=landed,
        device_id=(ctx, cache),
        device_id_type=MESH,
    )


def turn(i):
    return 0 if i == 0 else ((i + 1) // 2 if i % 2 else NZ - i // 2)


def greet(c, y, offsets):
    barrier = pltpu.get_barrier_semaphore()

    def ring(s, carry):
        pl.semaphore_signal(
            barrier, inc=1, device_id=(lax.rem(c + s, 2 * NX * NZ), y), device_id_type=MESH
        )
        return carry

    lax.fori_loop(1, 2 * NX * NZ, ring, 0)
    for o in offsets:
        pl.semaphore_signal(
            barrier, inc=1, device_id=(c, lax.rem(y + o, 4)), device_id_type=MESH
        )
    pl.semaphore_wait(barrier, 2 * NX * NZ - 1 + len(offsets))


def share(buf, sems, c, y, column, part, direct=()):
    sent, came, left, right, far = sems
    up = lax.rem(y + 1, 4)
    down = lax.rem(y + 3, 4)

    def piece(i, who):
        return buf.at[:, column(i), :, pl.ds(who * part, part), :]

    def forward(i):
        own = piece(i, y)
        going = push(own, own, sent.at[0, i], left.at[i], c, up)
        push(own, own, sent.at[0, i], came.at[i], c, up).wait_recv()
        going.start()
        push(own, own, sent.at[1, i], right.at[i], c, down).start()

    def relay(i):
        if i in direct:
            return
        if i % 2 == 0:
            got = piece(i, down)
            push(got, got, sent.at[2, i], left.at[i], c, up).wait_recv()
            push(got, got, sent.at[2, i], far.at[i], c, up).start()
        else:
            got = piece(i, up)
            push(got, got, sent.at[2, i], right.at[i], c, down).wait_recv()
            push(got, got, sent.at[2, i], far.at[i], c, down).start()

    def ready(i):
        if i % 2 == 0 or i in direct:
            got = piece(i, up)
            push(got, got, sent.at[2, i], right.at[i], c, down).wait_recv()
        if i % 2 or i in direct:
            got = piece(i, down)
            push(got, got, sent.at[2, i], left.at[i], c, up).wait_recv()
        got = piece(i, lax.rem(y + 2, 4))
        push(got, got, sent.at[2, i], far.at[i], c, up).wait_recv()

    def drain(i):
        own = piece(i, y)
        for k in range(2 if i in direct else 3):
            push(own, own, sent.at[k, i], far.at[i], c, up).wait_send()

    return forward, relay, ready, drain


def score(rows, keys):
    return lax.dot_general(
        keys, rows, (((1,), (1,)), ((), ())), preferred_element_type=jnp.float32
    )


def weigh_values(vals, probs):
    return lax.dot_general(
        vals, probs, (((0,), (0,)), ((), ())), preferred_element_type=jnp.float32
    )


def find_block(r, first, q0, q1, lists, owners, starts, k):
    held, lat, _ = k.shape
    images = owners.shape[0]
    slots = lists.shape[0] // 2
    sides = []
    for side in range(2):
        ids, gaps = [], []
        for s in range(slots):
            image = lists[side * slots + s, r]
            local = image - first
            owner = owners[jnp.minimum(image, images - 1)]
            here = (
                (image < images) & (owner == r - 1 + side) & (local >= 0) & (local < held)
            )
            ids.append(jnp.where(here, local, 0))
            gaps.append(jnp.where(here, 0.0, FAR))
        sides.append((ids, gaps))
    (old_ids, old_gaps), (ids, gaps) = sides
    keys = jnp.concatenate([k[i] for i in ids], axis=0)
    old_keys = jnp.concatenate([k[i] for i in old_ids], axis=0)
    new_scores = score(jnp.concatenate([q0, q1], axis=0), keys)
    old_scores = score(q0, old_keys)
    position = r * BLOCK + lax.broadcasted_iota(jnp.int32, (1, HD), 1)
    before = position < starts[r]
    return before, sides, new_scores, old_scores


def soften_block(state, slots, lat):
    before, sides, new_scores, old_scores = state
    (old_ids, old_gaps), (ids, gaps) = sides
    probs = []
    halves = []
    for half in range(2):
        tile = []
        levels = []
        top = jnp.full((1, HD), -FAR, jnp.float32)
        for s in range(slots):
            span = slice(s * lat, (s + 1) * lat)
            if half == 0:
                block = jnp.where(before, old_scores[span], new_scores[span, :HD])
                gap = jnp.where(before, old_gaps[s], gaps[s])
            else:
                block = new_scores[span, HD:]
                gap = jnp.full((1, HD), gaps[s], jnp.float32)
            tile.append(block)
            levels.append(gap)
            top = jnp.maximum(top, jnp.max(block, axis=0, keepdims=True) - gap)
        top = jnp.where(top < -0.5 * FAR, 0.0, top)
        total = jnp.zeros((1, HD), jnp.float32)
        weights = []
        for s in range(slots):
            p = jnp.exp2((tile[s] - (top + levels[s])) * SCALE2)
            total = total + jnp.sum(p, axis=0, keepdims=True)
            weights.append(p.astype(jnp.bfloat16))
        probs.append(jnp.concatenate(weights, axis=0))
        halves.append((top, total))
    return probs, halves


def mix_block(state, soft, v):
    before, sides, _, _ = state
    (old_ids, _), (ids, _) = sides
    probs, halves = soft
    vals = jnp.concatenate([v[i] for i in ids], axis=0)
    old_vals = jnp.concatenate([v[i] for i in old_ids], axis=0)
    summed = weigh_values(vals, jnp.concatenate(probs, axis=1))
    old_summed = weigh_values(old_vals, probs[0])
    results = []
    for half in range(2):
        top, total = halves[half]
        seen = total > 0
        safe = jnp.where(seen, total, 1.0)
        level = jnp.where(seen, top * SCALE2 + jnp.log2(safe), -FAR)
        numer = summed[:, half * HD : (half + 1) * HD]
        if half == 0:
            numer = jnp.where(before, old_summed, numer)
        results.append((level, (numer * (1.0 / safe)).astype(jnp.bfloat16)))
    return results


def whole_kernel(
    part, lists, owners, starts, q, k_hbm, v_hbm, result,
    buf, qbuf, k, v, own, levels, alpha, relayed, raw, added, adding, final,
    kv_sem, q_out, q_more, q_came, q_sent, q_left, q_right, q_far,
    l_sent, l_came, a_sent, a_came, r_sent, r_came, m_sent, m_came,
    o_out, o_came, o_sent, o_left, o_right, o_far,
):
    c = lax.axis_index("ctx")
    y = lax.axis_index("cache")
    x = c // (2 * NZ)
    z = lax.rem(c // 2, NZ)
    core = lax.rem(c, 2)
    up = lax.rem(y + 1, 4)
    down = lax.rem(y + 3, 4)
    across = lax.rem(y + 2, 4)
    first = y * k.shape[0]
    rows = pl.ds(y * part, part)
    loads = [
        pltpu.make_async_copy(k_hbm, k, kv_sem.at[0]),
        pltpu.make_async_copy(v_hbm, v, kv_sem.at[1]),
    ]
    for load in loads:
        load.start()
    greet(c, y, (1, 2, 3))

    def behind(i):
        return lax.rem(z + NZ - turn(i), NZ)

    def ahead(i):
        return lax.rem(z + turn(i), NZ)

    def everyone(one, i):
        def send(j, carry):
            to_x = lax.rem(x + j // 2, NX)
            to_core = lax.rem(core + lax.rem(j, 2), 2)
            one(to_x, to_core)
            return carry

        lax.fori_loop(1 if i == 0 else 0, 2 * NX, send, 0)

    def q_hand(i, who, out, came):
        span = pl.ds(pl.multiple_of(who * part, part), part)
        home = qbuf.at[x, z, core, span, :]

        def block(to):
            return q.at[span, pl.ds(pl.multiple_of(to * HD, HD), HD)]

        def q_send(to_x, to_core):
            to = to_x * (2 * NZ) + ahead(i) * 2 + to_core
            push(block(to), home, out.at[i], came.at[i], to, y).start()

        if i == 0:
            pltpu.make_async_copy(block(c), home, came.at[0]).start()
        everyone(q_send, i)

    for i in range(NZ):
        q_hand(i, y, q_out, q_came)
        if i in DIRECT:
            q_hand(i, across, q_more, q_far)
    q_forward, q_relay, q_ready, q_drain = share(
        qbuf, (q_sent, q_came, q_left, q_right, q_far), c, y, behind, part, DIRECT
    )

    def work(i):
        q_ready(i)
        if i == 0:
            for load in loads:
                load.wait()
        zs = behind(i)

        def some(g, carry):
            blocks = [g * PAIR + m for m in range(PAIR)]
            lat = k.shape[1]
            slots = lists.shape[0] // 2
            found = [
                find_block(
                    n * NZ + zs, first, qbuf[n, zs, 0], qbuf[n, zs, 1], lists, owners, starts, k
                )
                for n in blocks
            ]
            soft = [soften_block(found[0], slots, lat)]
            results = []
            for m in range(PAIR):
                if m + 1 < PAIR:
                    soft.append(soften_block(found[m + 1], slots, lat))
                results.append(mix_block(found[m], soft[m], v))
            for n, result in zip(blocks, results):
                for half in range(2):
                    level, block = result[half]
                    levels[y, i, n, :, half * HD : (half + 1) * HD] = level
                    own[i, n, :, half * HD : (half + 1) * HD] = block
            return carry

        lax.fori_loop(0, NX // PAIR, some, 0)

    def deep(who):
        return pl.ds(pl.multiple_of(who * part, part), part)

    low, high = pl.ds(0, 2), pl.ds(2, 2)
    tell = [
        [
            push(levels.at[y, i], levels.at[y, i], l_sent.at[o - 1, i], l_came.at[o - 1, i],
                 c, lax.rem(y + o, 4))
            for o in (1, 2, 3)
        ]
        for i in range(NZ)
    ]
    offers = [
        (
            push(own.at[i, low, deep(across), :], relayed.at[0, i],
                 a_sent.at[0, i], a_came.at[0, i], c, up),
            push(own.at[i, high, deep(across), :], relayed.at[1, i],
                 a_sent.at[1, i], a_came.at[1, i], c, down),
            push(own.at[i, high, deep(up), :], raw.at[0, i],
                 r_sent.at[0, i], r_came.at[0, i], c, up),
            push(own.at[i, low, deep(down), :], raw.at[1, i],
                 r_sent.at[1, i], r_came.at[1, i], c, down),
        )
        for i in range(NZ)
    ]
    adds = [
        (
            push(adding.at[0, i], added.at[0, i], m_sent.at[0, i], m_came.at[0, i], c, up),
            push(adding.at[1, i], added.at[1, i], m_sent.at[1, i], m_came.at[1, i], c, down),
        )
        for i in range(NZ)
    ]

    def offer(i):
        for p in tell[i] + list(offers[i]):
            p.start()

    def weigh(who, i, n, block):
        return block.astype(jnp.float32) * alpha[who, i, n]

    def add(i):
        for p in tell[i]:
            p.wait_recv()
        tops = jnp.maximum(
            jnp.maximum(levels[0, i], levels[1, i]), jnp.maximum(levels[2, i], levels[3, i])
        )
        weights = [jnp.exp2(levels[w, i] - tops) for w in range(4)]
        scale = 1.0 / (weights[0] + weights[1] + weights[2] + weights[3])
        for w in range(4):
            alpha[w, i] = weights[w] * scale
        offers[i][0].wait_recv()
        offers[i][1].wait_recv()
        for n in range(2):
            adding[0, i, n] = (
                weigh(down, i, n, relayed[0, i, n]) + weigh(y, i, n, own[i, n, deep(up), :])
            ).astype(jnp.bfloat16)
            adding[1, i, n] = (
                weigh(up, i, n + 2, relayed[1, i, n])
                + weigh(y, i, n + 2, own[i, n + 2, deep(down), :])
            ).astype(jnp.bfloat16)

    def complete(i):
        offers[i][2].wait_recv()
        offers[i][3].wait_recv()
        for p in adds[i]:
            p.wait_recv()
        for n in range(2):
            final[i, n] = (
                weigh(y, i, n, own[i, n, deep(y), :])
                + added[0, i, n].astype(jnp.float32)
                + weigh(up, i, n, raw[1, i, n])
            ).astype(jnp.bfloat16)
            final[i, n + 2] = (
                weigh(y, i, n + 2, own[i, n + 2, deep(y), :])
                + added[1, i, n].astype(jnp.float32)
                + weigh(down, i, n + 2, raw[0, i, n])
            ).astype(jnp.bfloat16)

    o_home = buf.at[x, z, core, rows, :]

    def o_block(i, to_x, to_core):
        return final.at[i, to_x, :, pl.ds(pl.multiple_of(to_core * HD, HD), HD)]

    def scatter(i):
        def o_send(to_x, to_core):
            to = to_x * (2 * NZ) + behind(i) * 2 + to_core
            push(o_block(i, to_x, to_core), o_home, o_out.at[i], o_came.at[i], to, y).start()

        if i == 0:
            pltpu.make_async_copy(o_block(0, x, core), o_home, o_came.at[0]).start()
        everyone(o_send, i)

    o_forward, o_relay, o_ready, o_drain = share(
        buf, (o_sent, o_came, o_left, o_right, o_far), c, y, ahead, part
    )

    row = lax.broadcasted_iota(jnp.int32, (HD, HD), 0)
    column = lax.broadcasted_iota(jnp.int32, (HD, HD), 1)
    unit = (row == column).astype(jnp.bfloat16)

    def turned(i):
        o_ready(i)
        zs = ahead(i)
        for n in range(NX):
            heads = buf[n, zs].reshape(2 * HD, HD)
            to = pl.multiple_of((n * NZ + zs) * 2 * HD, 2 * HD)
            result[:, pl.ds(to, 2 * HD)] = score(heads, unit).astype(jnp.bfloat16)

    def settle(i):
        for p in tell[i] + list(offers[i]) + list(adds[i]):
            p.wait_send()
        for which, out, came in ((q_drain, q_out, q_came), (o_drain, o_out, o_came)):
            which(i)
            if i == 0:
                some = buf.at[0, pl.ds(0, 2 * NX - 1), 0, pl.ds(0, part), :]
            else:
                some = buf.at[0, :, 0, pl.ds(0, part), :]
            push(some, some, out.at[i], came.at[i], c, y).wait_send()
            if i in DIRECT and which is q_drain:
                push(some, some, q_more.at[i], came.at[i], c, y).wait_send()

    def at(t, lag):
        return 0 <= t - lag < NZ

    for t in range(NZ + TURN):
        if at(t, 0):
            q_forward(t)
        if at(t, RELAY):
            q_relay(t - RELAY)
        if at(t, WORK):
            work(t - WORK)
        if at(t, ADD):
            add(t - ADD)
        if at(t, DONE):
            complete(t - DONE)
        if at(t, WORK):
            offer(t - WORK)
        if at(t, ADD):
            for p in adds[t - ADD]:
                p.start()
        if at(t, DONE):
            scatter(t - DONE)
        if at(t, ONWARD):
            o_forward(t - ONWARD)
        if at(t, LAST):
            o_relay(t - LAST)
        if at(t, TURN):
            turned(t - TURN)
            settle(t - TURN)


def whole(queries, keys, values, lists, img_req, req_start, part):
    def kernel(*refs):
        whole_kernel(part, *refs)

    dma = pltpu.SemaphoreType.DMA
    smem = pl.BlockSpec(memory_space=pltpu.SMEM)
    far = pl.BlockSpec(memory_space=pl.ANY)
    half = pltpu.VMEM((2, NZ, 2, part, BLOCK), jnp.bfloat16)
    heads = (NX, NZ, 2, HD, HD)
    level = pltpu.VMEM((4, NZ, NX, 1, BLOCK), jnp.float32)
    one, two, three = dma((NZ,)), dma((2, NZ)), dma((3, NZ))
    return pl.pallas_call(
        kernel,
        out_shape=pltpu.VMEM((queries.shape[0], queries.shape[1]), jnp.bfloat16),
        in_specs=[smem, smem, smem, far, far, far],
        out_specs=pl.BlockSpec(memory_space=pltpu.VMEM),
        scratch_shapes=[
            pltpu.VMEM(heads, jnp.bfloat16),
            pltpu.VMEM(heads, jnp.bfloat16),
            pltpu.VMEM(keys.shape, jnp.bfloat16),
            pltpu.VMEM(keys.shape, jnp.bfloat16),
            pltpu.VMEM((NZ, NX, HD, BLOCK), jnp.bfloat16),
            level, level, half, half, half, half,
            pltpu.VMEM((NZ, NX, part, BLOCK), jnp.bfloat16),
            dma((2,)), one, one, one, three, one, one, one,
            three, three, two, two, two, two, two, two,
            one, one, three, one, one, one,
        ],
        compiler_params=pltpu.CompilerParams(collective_id=1, has_side_effects=True),
        name="whole",
    )(lists, img_req, req_start, queries, keys, values)


def shards(queries, keys, values, block_imgs, img_req, req_start):
    part = queries.shape[0] // lax.axis_size("cache")
    return whole(queries, keys, values, block_imgs.T, img_req, req_start, part)


def solution(mesh):
    placed = (P("ctx", None), P("cache", None, "ctx"), P("cache", None, "ctx"), P(), P(), P())
    return jax.shard_map(
        shards, mesh=mesh, in_specs=placed, out_specs=P("ctx", None), check_vma=False
    )
```

```python
import jax
import jax.numpy as jnp
from jax import lax
from jax.experimental import pallas as pl
from jax.experimental.pallas import tpu as pltpu
from jax.sharding import PartitionSpec as P

HD = 128
BLOCK = 256
NX = 4
NZ = 8
FAR = 1e30
SCALE2 = HD ** (-0.5) * 1.4426950408889634
MESH = pl.DeviceIdType.MESH
RELAY, WORK, ADD, DONE, ONWARD, LAST, TURN = 1, 2, 5, 8, 11, 13, 15
DIRECT = (0, 1, 2, 3, 4, 5, 6, 7)
PAIR = 4


def push(src, dst, sent, landed, ctx, cache):
    return pltpu.make_async_remote_copy(
        src_ref=src,
        dst_ref=dst,
        send_sem=sent,
        recv_sem=landed,
        device_id=(ctx, cache),
        device_id_type=MESH,
    )


def turn(i):
    return (1, 7, 2, 6, 3, 5, 4, 0)[i]


def hops(shift):
    dx, dz, _ = shift
    return min(dx, NX - dx) + min(dz, NZ - dz)


def greet(c, y, offsets):
    barrier = pltpu.get_barrier_semaphore()
    xs = [lax.rem(c // (2 * NZ) + d, NX) * (2 * NZ) for d in range(NX)]
    zs = [lax.rem(c // 2 + d, NZ) * 2 for d in range(NZ)]
    cores = [lax.rem(c + d, 2) for d in range(2)]
    shifts = [(dx, dz, dc) for dx in range(NX) for dz in range(NZ) for dc in range(2)]
    for dx, dz, dc in sorted(shifts[1:], key=hops, reverse=True):
        pl.semaphore_signal(
            barrier, inc=1, device_id=(xs[dx] + zs[dz] + cores[dc], y), device_id_type=MESH
        )
    for o in offsets:
        pl.semaphore_signal(
            barrier, inc=1, device_id=(c, lax.rem(y + o, 4)), device_id_type=MESH
        )
    pl.semaphore_wait(barrier, 2 * NX * NZ - 1 + len(offsets))


def share(buf, sems, c, y, column, part, direct=()):
    sent, came, left, right, far = sems
    up = lax.rem(y + 1, 4)
    down = lax.rem(y + 3, 4)

    def piece(i, who):
        return buf.at[:, column(i), :, pl.ds(who * part, part), :]

    def forward(i):
        own = piece(i, y)
        going = push(own, own, sent.at[0, i], left.at[i], c, up)
        push(own, own, sent.at[0, i], came.at[i], c, up).wait_recv()
        going.start()
        push(own, own, sent.at[1, i], right.at[i], c, down).start()

    def relay(i):
        if i in direct:
            return
        if i % 2 == 0:
            got = piece(i, down)
            push(got, got, sent.at[2, i], left.at[i], c, up).wait_recv()
            push(got, got, sent.at[2, i], far.at[i], c, up).start()
        else:
            got = piece(i, up)
            push(got, got, sent.at[2, i], right.at[i], c, down).wait_recv()
            push(got, got, sent.at[2, i], far.at[i], c, down).start()

    def ready(i):
        if i % 2 == 0 or i in direct:
            got = piece(i, up)
            push(got, got, sent.at[2, i], right.at[i], c, down).wait_recv()
        if i % 2 or i in direct:
            got = piece(i, down)
            push(got, got, sent.at[2, i], left.at[i], c, up).wait_recv()
        got = piece(i, lax.rem(y + 2, 4))
        push(got, got, sent.at[2, i], far.at[i], c, up).wait_recv()

    def drain(i):
        own = piece(i, y)
        for k in range(2 if i in direct else 3):
            push(own, own, sent.at[k, i], far.at[i], c, up).wait_send()

    return forward, relay, ready, drain


def score(rows, keys):
    return lax.dot_general(
        keys, rows, (((1,), (1,)), ((), ())), preferred_element_type=jnp.float32
    )


def weigh_values(vals, probs):
    return lax.dot_general(
        vals, probs, (((0,), (0,)), ((), ())), preferred_element_type=jnp.float32
    )


def find_block(r, first, q0, q1, lists, owners, starts, k):
    held, lat, _ = k.shape
    images = owners.shape[0]
    slots = lists.shape[0] // 2
    sides = []
    for side in range(2):
        ids, gaps = [], []
        for s in range(slots):
            image = lists[side * slots + s, r]
            local = image - first
            owner = owners[jnp.minimum(image, images - 1)]
            here = (
                (image < images) & (owner == r - 1 + side) & (local >= 0) & (local < held)
            )
            ids.append(jnp.where(here, local, 0))
            gaps.append(jnp.where(here, 0.0, FAR))
        sides.append((ids, gaps))
    (old_ids, old_gaps), (ids, gaps) = sides
    keys = jnp.concatenate([k[i] for i in ids], axis=0)
    old_keys = jnp.concatenate([k[i] for i in old_ids], axis=0)
    new_scores = score(jnp.concatenate([q0, q1], axis=0), keys)
    old_scores = score(q0, old_keys)
    position = r * BLOCK + lax.broadcasted_iota(jnp.int32, (1, HD), 1)
    before = position < starts[r]
    return before, sides, new_scores, old_scores


def soften_block(state, slots, lat):
    before, sides, new_scores, old_scores = state
    (old_ids, old_gaps), (ids, gaps) = sides
    probs = []
    halves = []
    for half in range(2):
        tile = []
        levels = []
        top = jnp.full((1, HD), -FAR, jnp.float32)
        for s in range(slots):
            span = slice(s * lat, (s + 1) * lat)
            if half == 0:
                block = jnp.where(before, old_scores[span], new_scores[span, :HD])
                gap = jnp.where(before, old_gaps[s], gaps[s])
            else:
                block = new_scores[span, HD:]
                gap = jnp.full((1, HD), gaps[s], jnp.float32)
            tile.append(block)
            levels.append(gap)
            top = jnp.maximum(top, jnp.max(block, axis=0, keepdims=True) - gap)
        top = jnp.where(top < -0.5 * FAR, 0.0, top)
        total = jnp.zeros((1, HD), jnp.float32)
        weights = []
        for s in range(slots):
            p = jnp.exp2((tile[s] - (top + levels[s])) * SCALE2)
            total = total + jnp.sum(p, axis=0, keepdims=True)
            weights.append(p.astype(jnp.bfloat16))
        probs.append(jnp.concatenate(weights, axis=0))
        halves.append((top, total))
    return probs, halves


def mix_block(state, soft, v):
    before, sides, _, _ = state
    (old_ids, _), (ids, _) = sides
    probs, halves = soft
    vals = jnp.concatenate([v[i] for i in ids], axis=0)
    old_vals = jnp.concatenate([v[i] for i in old_ids], axis=0)
    summed = weigh_values(vals, jnp.concatenate(probs, axis=1))
    old_summed = weigh_values(old_vals, probs[0])
    results = []
    for half in range(2):
        top, total = halves[half]
        seen = total > 0
        safe = jnp.where(seen, total, 1.0)
        level = jnp.where(seen, top * SCALE2 + jnp.log2(safe), -FAR)
        numer = summed[:, half * HD : (half + 1) * HD]
        if half == 0:
            numer = jnp.where(before, old_summed, numer)
        results.append((level, (numer * (1.0 / safe)).astype(jnp.bfloat16)))
    return results


def whole_kernel(
    part, lists, owners, starts, q, k_hbm, v_hbm, result,
    buf, qbuf, k, v, own, levels, alpha, relayed, raw, added, adding, final,
    kv_sem, q_out, q_more, q_came, q_sent, q_left, q_right, q_far,
    l_sent, l_came, a_sent, a_came, r_sent, r_came, m_sent, m_came,
    o_out, o_came, o_sent, o_left, o_right, o_far,
):
    c = lax.axis_index("ctx")
    y = lax.axis_index("cache")
    x = c // (2 * NZ)
    z = lax.rem(c // 2, NZ)
    core = lax.rem(c, 2)
    up = lax.rem(y + 1, 4)
    down = lax.rem(y + 3, 4)
    across = lax.rem(y + 2, 4)
    first = y * k.shape[0]
    rows = pl.ds(y * part, part)
    loads = [
        pltpu.make_async_copy(k_hbm, k, kv_sem.at[0]),
        pltpu.make_async_copy(v_hbm, v, kv_sem.at[1]),
    ]
    for load in loads:
        load.start()
    greet(c, y, (1, 2, 3))

    def behind(i):
        return lax.rem(z + NZ - turn(i), NZ)

    def ahead(i):
        return lax.rem(z + turn(i), NZ)

    xs = [lax.rem(x + d, NX) for d in range(NX)]
    cores = [lax.rem(core + d, 2) for d in range(2)]

    def everyone(one, i):
        for j in range(1 if turn(i) == 0 else 0, 2 * NX):
            one(xs[j // 2], cores[j % 2])

    def q_hand(i, who, out, came):
        span = pl.ds(pl.multiple_of(who * part, part), part)
        home = qbuf.at[x, z, core, span, :]

        def block(to):
            return q.at[span, pl.ds(pl.multiple_of(to * HD, HD), HD)]

        def q_send(to_x, to_core):
            to = to_x * (2 * NZ) + ahead(i) * 2 + to_core
            push(block(to), home, out.at[i], came.at[i], to, y).start()

        if turn(i) == 0:
            pltpu.make_async_copy(block(c), home, came.at[i]).start()
        everyone(q_send, i)

    for i in range(NZ):
        q_hand(i, y, q_out, q_came)
        if i in DIRECT:
            q_hand(i, across, q_more, q_far)
    q_forward, q_relay, q_ready, q_drain = share(
        qbuf, (q_sent, q_came, q_left, q_right, q_far), c, y, behind, part, DIRECT
    )

    def work(i):
        q_ready(i)
        if i == 0:
            for load in loads:
                load.wait()
        zs = behind(i)

        def some(g, carry):
            blocks = [g * PAIR + m for m in range(PAIR)]
            lat = k.shape[1]
            slots = lists.shape[0] // 2
            found = [
                find_block(
                    n * NZ + zs, first, qbuf[n, zs, 0], qbuf[n, zs, 1], lists, owners, starts, k
                )
                for n in blocks
            ]
            soft = [soften_block(found[0], slots, lat)]
            results = []
            for m in range(PAIR):
                if m + 1 < PAIR:
                    soft.append(soften_block(found[m + 1], slots, lat))
                results.append(mix_block(found[m], soft[m], v))
            for n, result in zip(blocks, results):
                for half in range(2):
                    level, block = result[half]
                    levels[y, i, n, :, half * HD : (half + 1) * HD] = level
                    own[i, n, :, half * HD : (half + 1) * HD] = block
            return carry

        lax.fori_loop(0, NX // PAIR, some, 0)

    def deep(who):
        return pl.ds(pl.multiple_of(who * part, part), part)

    low, high = pl.ds(0, 2), pl.ds(2, 2)
    tell = [
        [
            push(levels.at[y, i], levels.at[y, i], l_sent.at[o - 1, i], l_came.at[o - 1, i],
                 c, lax.rem(y + o, 4))
            for o in (1, 2, 3)
        ]
        for i in range(NZ)
    ]
    offers = [
        (
            push(own.at[i, low, deep(across), :], relayed.at[0, i],
                 a_sent.at[0, i], a_came.at[0, i], c, up),
            push(own.at[i, high, deep(across), :], relayed.at[1, i],
                 a_sent.at[1, i], a_came.at[1, i], c, down),
            push(own.at[i, high, deep(up), :], raw.at[0, i],
                 r_sent.at[0, i], r_came.at[0, i], c, up),
            push(own.at[i, low, deep(down), :], raw.at[1, i],
                 r_sent.at[1, i], r_came.at[1, i], c, down),
        )
        for i in range(NZ)
    ]
    adds = [
        (
            push(adding.at[0, i], added.at[0, i], m_sent.at[0, i], m_came.at[0, i], c, up),
            push(adding.at[1, i], added.at[1, i], m_sent.at[1, i], m_came.at[1, i], c, down),
        )
        for i in range(NZ)
    ]

    def offer(i):
        for p in tell[i] + list(offers[i]):
            p.start()

    def weigh(who, i, n, block):
        return block.astype(jnp.float32) * alpha[who, i, n]

    def add(i):
        for p in tell[i]:
            p.wait_recv()
        tops = jnp.maximum(
            jnp.maximum(levels[0, i], levels[1, i]), jnp.maximum(levels[2, i], levels[3, i])
        )
        weights = [jnp.exp2(levels[w, i] - tops) for w in range(4)]
        scale = 1.0 / (weights[0] + weights[1] + weights[2] + weights[3])
        for w in range(4):
            alpha[w, i] = weights[w] * scale
        offers[i][0].wait_recv()
        offers[i][1].wait_recv()
        for n in range(2):
            adding[0, i, n] = (
                weigh(down, i, n, relayed[0, i, n]) + weigh(y, i, n, own[i, n, deep(up), :])
            ).astype(jnp.bfloat16)
            adding[1, i, n] = (
                weigh(up, i, n + 2, relayed[1, i, n])
                + weigh(y, i, n + 2, own[i, n + 2, deep(down), :])
            ).astype(jnp.bfloat16)

    def complete(i):
        offers[i][2].wait_recv()
        offers[i][3].wait_recv()
        for p in adds[i]:
            p.wait_recv()
        for n in range(2):
            final[i, n] = (
                weigh(y, i, n, own[i, n, deep(y), :])
                + added[0, i, n].astype(jnp.float32)
                + weigh(up, i, n, raw[1, i, n])
            ).astype(jnp.bfloat16)
            final[i, n + 2] = (
                weigh(y, i, n + 2, own[i, n + 2, deep(y), :])
                + added[1, i, n].astype(jnp.float32)
                + weigh(down, i, n + 2, raw[0, i, n])
            ).astype(jnp.bfloat16)

    o_home = buf.at[x, z, core, rows, :]

    def o_block(i, to_x, to_core):
        return final.at[i, to_x, :, pl.ds(pl.multiple_of(to_core * HD, HD), HD)]

    def scatter(i):
        def o_send(to_x, to_core):
            to = to_x * (2 * NZ) + behind(i) * 2 + to_core
            push(o_block(i, to_x, to_core), o_home, o_out.at[i], o_came.at[i], to, y).start()

        if turn(i) == 0:
            pltpu.make_async_copy(o_block(i, x, core), o_home, o_came.at[i]).start()
        everyone(o_send, i)

    o_forward, o_relay, o_ready, o_drain = share(
        buf, (o_sent, o_came, o_left, o_right, o_far), c, y, ahead, part
    )

    row = lax.broadcasted_iota(jnp.int32, (HD, HD), 0)
    column = lax.broadcasted_iota(jnp.int32, (HD, HD), 1)
    unit = (row == column).astype(jnp.bfloat16)

    def turned(i):
        o_ready(i)
        zs = ahead(i)
        for n in range(NX):
            heads = buf[n, zs].reshape(2 * HD, HD)
            to = pl.multiple_of((n * NZ + zs) * 2 * HD, 2 * HD)
            result[:, pl.ds(to, 2 * HD)] = score(heads, unit).astype(jnp.bfloat16)

    def settle(i):
        for p in tell[i] + list(offers[i]) + list(adds[i]):
            p.wait_send()
        for which, out, came in ((q_drain, q_out, q_came), (o_drain, o_out, o_came)):
            which(i)
            if turn(i) == 0:
                some = buf.at[0, pl.ds(0, 2 * NX - 1), 0, pl.ds(0, part), :]
            else:
                some = buf.at[0, :, 0, pl.ds(0, part), :]
            push(some, some, out.at[i], came.at[i], c, y).wait_send()
            if i in DIRECT and which is q_drain:
                push(some, some, q_more.at[i], came.at[i], c, y).wait_send()

    def at(t, lag):
        return 0 <= t - lag < NZ

    for t in range(NZ + TURN):
        if at(t, 0):
            q_forward(t)
        if at(t, RELAY):
            q_relay(t - RELAY)
        if at(t, WORK):
            work(t - WORK)
        if at(t, ADD):
            add(t - ADD)
        if at(t, DONE):
            complete(t - DONE)
        if at(t, WORK):
            offer(t - WORK)
        if at(t, ADD):
            for p in adds[t - ADD]:
                p.start()
        if at(t, DONE):
            scatter(t - DONE)
        if at(t, ONWARD):
            o_forward(t - ONWARD)
        if at(t, LAST):
            o_relay(t - LAST)
        if at(t, TURN):
            turned(t - TURN)
            settle(t - TURN)


def whole(queries, keys, values, lists, img_req, req_start, part):
    def kernel(*refs):
        whole_kernel(part, *refs)

    dma = pltpu.SemaphoreType.DMA
    smem = pl.BlockSpec(memory_space=pltpu.SMEM)
    far = pl.BlockSpec(memory_space=pl.ANY)
    half = pltpu.VMEM((2, NZ, 2, part, BLOCK), jnp.bfloat16)
    heads = (NX, NZ, 2, HD, HD)
    level = pltpu.VMEM((4, NZ, NX, 1, BLOCK), jnp.float32)
    one, two, three = dma((NZ,)), dma((2, NZ)), dma((3, NZ))
    return pl.pallas_call(
        kernel,
        out_shape=pltpu.VMEM((queries.shape[0], queries.shape[1]), jnp.bfloat16),
        in_specs=[smem, smem, smem, far, far, far],
        out_specs=pl.BlockSpec(memory_space=pltpu.VMEM),
        scratch_shapes=[
            pltpu.VMEM(heads, jnp.bfloat16),
            pltpu.VMEM(heads, jnp.bfloat16),
            pltpu.VMEM(keys.shape, jnp.bfloat16),
            pltpu.VMEM(keys.shape, jnp.bfloat16),
            pltpu.VMEM((NZ, NX, HD, BLOCK), jnp.bfloat16),
            level, level, half, half, half, half,
            pltpu.VMEM((NZ, NX, part, BLOCK), jnp.bfloat16),
            dma((2,)), one, one, one, three, one, one, one,
            three, three, two, two, two, two, two, two,
            one, one, three, one, one, one,
        ],
        compiler_params=pltpu.CompilerParams(collective_id=1, has_side_effects=True),
        name="whole",
    )(lists, img_req, req_start, queries, keys, values)


def shards(queries, keys, values, block_imgs, img_req, req_start):
    part = queries.shape[0] // lax.axis_size("cache")
    return whole(queries, keys, values, block_imgs.T, img_req, req_start, part)


def solution(mesh):
    placed = (P("ctx", None), P("cache", None, "ctx"), P("cache", None, "ctx"), P(), P(), P())
    return jax.shard_map(
        shards, mesh=mesh, in_specs=placed, out_specs=P("ctx", None), check_vma=False
    )
```
